32 devices in a mesh: grp: 2 (over x), yz: 8 (over z, y), gx: 2 (over core).
Axes of the slice: x: 2, y: 2, z: 4, core: 2. Of those that a mesh axis runs over, the one named last changes fastest.
Arguments:
- field: bfloat16 [4096, 256, 128], P(('grp', 'gx'), 'yz'), parts along dimension 0, may hold values from -6 to 6
- sketch_seeds: int32 [12], P('grp'), parts along dimension 0, may hold values from 1 to 32748
Outputs:
- basis: float32 [4096, 256], P(('grp', 'gx')), parts along dimension 0
- core: bfloat16 [512, 256, 128], P(('grp', 'gx'), 'yz'), parts along dimension 0
The draws below stay inside these ranges and needn't reach their ends.
There are 2 independent parts, one for each index of `grp`. The reference program is written for one: setup_inputs(seed, part) draws one part's arguments, and reference() takes and returns one part's arrays. A program takes and returns all parts, laid end to end along the dimension named above; each array names one. Nothing has to cross between parts.
All inputs are finite; a program needn't handle non-finite values.
Results may differ from the reference program's by a relative error of at most 0.0057.
Values sent between devices are 32-bit elements; how exact they have to be, the bound alone decides.
No kernel may reach another device: no remote copies, remote signals or barrier semaphores. Data moves between devices by JAX's collectives and lax.ppermute only.
A program may use at most 64 MiB of HBM per device.

```python
import math
import jax
import jax.numpy as jnp
from jax import lax

XR = 2048
RANK = 256
ZS = 128
YN = 256


def with_ends(array, key, least, largest):
    spot = [jax.random.randint(jax.random.fold_in(key, axis), (), 0, length) for axis, length in enumerate(array.shape)]
    widest = array.shape.index(max(array.shape))
    beside = spot[:widest] + [(spot[widest] + 1) % array.shape[widest]] + spot[widest + 1:]
    return array.at[tuple(spot)].set(least).at[tuple(beside)].set(largest)


def steps_of(own_key, dims, cuts, smallest, high):
    loudness, own = 1.0, jax.random.fold_in(own_key, 6)
    for position, blocks in cuts:
        draws = jnp.exp(jax.random.uniform(jax.random.fold_in(own, position), (blocks,), jnp.float32, smallest / len(cuts), high / len(cuts)))
        loudness = loudness * jnp.repeat(draws, dims[position] // blocks).reshape([-1 if axis == position else 1 for axis in range(len(dims))])
    return loudness


def scatter_about(stream_key, extent, scale, most, pieces=(), held_as=jnp.bfloat16):
    array = jax.random.normal(stream_key, extent, jnp.float32) * scale
    if len(pieces) > 0:
        array = steps_of(stream_key, extent, pieces, -0.22, 0.18) * array
    return jnp.clip(array, min=-most, max=most).astype(held_as)


def setup_inputs(seed: int = 0, part: int = 0) -> dict:
    key_of = jax.random.split(jax.random.key(seed), 3)
    own_keys = jax.random.split(jax.random.fold_in(key_of[2], part), 3)
    return {
        "field": scatter_about(own_keys[0], (XR, YN, ZS), 1.0, 6.0, ((0, 2), (1, 8))),
        "sketch_seeds": with_ends(jax.random.randint(own_keys[1], (6,), 1, 32749), jax.random.fold_in(own_keys[1], 1), 1, 32748).astype(jnp.int32),
    }


prime = 32749

def omega_table(seeds, start, count):
    place = (start + jnp.arange(count, dtype=jnp.int32) + 1).astype(jnp.int32)[:, None]
    column = (jnp.arange(RANK, dtype=jnp.int32) + 1)[None, :]
    first = seeds[0] * place % prime
    second = (seeds[1] * column + seeds[2]) % prime
    square = place * place % prime
    third = seeds[2] * column % prime
    mixed = (first * second % prime + square * third % prime) % prime
    return mixed.astype(jnp.float32) * (2.0 / prime) - 1.0

def reference(field, sketch_seeds):
    omega_z = omega_table(sketch_seeds[3:6], 0, ZS).astype(jnp.bfloat16).astype(jnp.float32)
    block = math.gcd(YN, 8)

    def add_block(total, index):
        rows = lax.dynamic_slice_in_dim(field, (index * block).astype(jnp.int32), block, 1).astype(jnp.float32)
        proj = jnp.dot(rows.reshape(XR * block, ZS).astype(jnp.float32), omega_z.astype(jnp.float32), precision=lax.Precision.HIGHEST, preferred_element_type=jnp.float32).reshape(XR, block, RANK)
        weight_y = omega_table(sketch_seeds[0:3], (index * block).astype(jnp.int32), block)
        return (total + jnp.sum(proj * weight_y[None], axis=1), None)
    sketch, unused = lax.scan(add_block, jnp.zeros((XR, RANK), jnp.float32), jnp.arange(YN // block, dtype=jnp.int32))
    gram = jnp.dot(sketch.T.astype(jnp.float32), sketch.astype(jnp.float32), precision=lax.Precision.HIGHEST, preferred_element_type=jnp.float32)
    lower = jnp.linalg.cholesky(gram)
    basis = lax.linalg.triangular_solve(lower, sketch, left_side=False, lower=True, transpose_a=True)
    basis_half = basis.astype(jnp.bfloat16).astype(jnp.float32)
    flat = field.reshape(XR, YN * ZS).astype(jnp.float32)
    core = jnp.dot(basis_half.T.astype(jnp.float32), flat.astype(jnp.float32), precision=lax.Precision.HIGHEST, preferred_element_type=jnp.float32)
    return (basis, core.reshape(RANK, YN, ZS).astype(jnp.bfloat16))
```

```python
import jax
import jax.numpy as jnp
from jax import lax
from jax.experimental import pallas as pl
from jax.experimental.pallas import tpu as pltpu
from jax.sharding import PartitionSpec as P

RANK = 256
prime = 32749
f32, bf16, i32 = jnp.float32, jnp.bfloat16, jnp.int32


def remainder(value):
    quotient = (value.astype(f32) * (1.0 / prime)).astype(i32)
    rest = value - quotient * prime
    rest = jnp.where(rest < 0, rest + prime, rest)
    return jnp.where(rest >= prime, rest - prime, rest)


def omega_table(a, b, c, start, count):
    place = start + 1 + lax.broadcasted_iota(i32, (count, 1), 0)
    column = 1 + lax.broadcasted_iota(i32, (1, RANK), 1)
    first = remainder(a * place)
    second = remainder(b * column + c)
    square = remainder(place * place)
    third = remainder(c * column)
    mixed = remainder(remainder(first * second) + remainder(square * third))
    return mixed.astype(f32) * (2.0 / prime) - 1.0


def sketch_kernel(scal, send_rows, keep_rows, send_out, keep_out, omega_z, omega_y):
    _, y_local, z_local = send_rows.shape
    omega_z[...] = omega_table(scal[4], scal[5], scal[6], 0, z_local).astype(bf16)
    omega_y[...] = omega_table(scal[1], scal[2], scal[3], scal[0], y_local)
    table_z, weight_y = omega_z[...], omega_y[...]
    sub = 16
    for rows, out in ((send_rows, send_out), (keep_rows, keep_out)):
        for start in range(0, rows.shape[0], sub):
            block = rows[start:start + sub].reshape(sub * y_local, z_local)
            proj = jnp.dot(block, table_z, preferred_element_type=f32)
            proj = proj.reshape(sub, y_local, RANK) * weight_y[None]
            out[start:start + sub, :] = jnp.sum(proj, axis=1)


def sketch_pair(field, scal, chunk):
    _, y_local, z_local = field.shape
    shape = jax.ShapeDtypeStruct((chunk, RANK), f32)
    return pl.pallas_call(
        sketch_kernel,
        grid_spec=pltpu.PrefetchScalarGridSpec(
            num_scalar_prefetch=1,
            grid=(1,),
            in_specs=[
                pl.BlockSpec((chunk, y_local, z_local), lambda i, s: (s[7], 0, 0)),
                pl.BlockSpec((chunk, y_local, z_local), lambda i, s: (s[8], 0, 0)),
            ],
            out_specs=[pl.BlockSpec((chunk, RANK), lambda i, s: (0, 0))] * 2,
            scratch_shapes=[pltpu.VMEM((z_local, RANK), bf16), pltpu.VMEM((y_local, RANK), f32)],
        ),
        out_shape=(shape, shape),
        name="sketch",
    )(scal, field, field)


def split3(value):
    high = value.astype(bf16)
    rest = value - high.astype(f32)
    middle = rest.astype(bf16)
    return high, middle, (rest - middle.astype(f32)).astype(bf16)


PANEL = 32


def inverse_factor_kernel(gram, out, state):
    size = gram.shape[0]
    state[...] = gram[...]
    lane = lax.broadcasted_iota(i32, (PANEL, 128), 1)
    row = lax.broadcasted_iota(i32, (PANEL, 128), 0)
    for low in range(0, size, PANEL):
        high = low + PANEL
        tile, offset = low // 128, low % 128
        rows = [state[low:high, 0:128], state[low:high, 128:256]]
        rows.append(jnp.where(lane == row + offset, 1.0, 0.0).astype(f32))
        done = [[None] * PANEL for _ in rows]
        for i in range(0, PANEL, 2):
            first = jnp.broadcast_to(rows[tile][:, offset + i:offset + i + 1], (PANEL, 128))
            second = jnp.broadcast_to(rows[tile][:, offset + i + 1:offset + i + 2], (PANEL, 128))
            d11, d12, d22 = first[i:i + 1], second[i:i + 1], second[i + 1:i + 2]
            scale = 1.0 / (d11 * d22 - d12 * d12)
            k11, k12, k22 = d22 * scale, d12 * scale, d11 * scale
            first = jnp.where(row > i + 1, first, 0.0)
            second = jnp.where(row > i + 1, second, 0.0)
            ratio = d12 / d11
            root1, root2 = lax.rsqrt(d11), lax.rsqrt(d22 - ratio * d12)
            for k in range(3):
                upper, lower = rows[k][i:i + 1], rows[k][i + 1:i + 2]
                done[k][i] = upper * root1
                done[k][i + 1] = (lower - ratio * upper) * root2
                if i + 2 < PANEL:
                    rows[k] = rows[k] - (
                        first * (k11 * upper - k12 * lower) + second * (k22 * lower - k12 * upper)
                    )
        factor = [jnp.concatenate(part, axis=0) for part in done]
        inside = (lane >= offset) & (lane < offset + PANEL)
        mixed = list(factor[:2])
        mixed[tile] = jnp.where(inside, factor[2], factor[tile])
        for k in range(2):
            if k < tile:
                value = mixed[k]
            elif k == tile:
                value = jnp.where(lane < offset + PANEL, mixed[k], 0.0)
            else:
                value = jnp.zeros((PANEL, 128), f32)
            out[low:high, 128 * k:128 * (k + 1)] = value
        if high < size:
            h, m, l = split3(jnp.concatenate(factor[:2], axis=1))
            eh, em, el = split3(jnp.concatenate(mixed, axis=1))
            left = jnp.concatenate([h, h, m, m, h, l], axis=0)
            right = jnp.concatenate([eh, em, eh, em, el, eh], axis=0)
            update = lax.dot_general(
                left, right, (((0,), (0,)), ((), ())), preferred_element_type=f32
            )
            lanes = lax.broadcasted_iota(i32, (size - high, size), 1)
            rest = jnp.where((lanes >= low) & (lanes < high), 0.0, state[high:, :])
            state[high:, :] = rest - update[high:, :]


def inverse_factor(gram):
    return pl.pallas_call(
        inverse_factor_kernel,
        out_shape=jax.ShapeDtypeStruct(gram.shape, f32),
        scratch_shapes=[pltpu.VMEM(gram.shape, f32)],
        name="inverse_factor",
    )(gram)


def local(field, sketch_seeds):
    x_local, y_local, z_local = field.shape
    count = lax.axis_size("yz")
    inner = 2 if count % 2 == 0 else 1
    outer = count // inner
    chunk = x_local // count
    here = lax.axis_index("yz")
    o, y = here // inner, here % inner

    def neighbour(value):
        return lax.ppermute(value, "yz", [(i, i ^ 1) for i in range(count)])

    def shift(value, d):
        pairs = [(i, (i // inner + d) % outer * inner + i % inner) for i in range(count)]
        return lax.ppermute(value, "yz", pairs)

    def other_core(value):
        return lax.ppermute(value, "gx", [(0, 1), (1, 0)])

    order = list(range(1, outer)) + [0]
    own = None
    for d in order:
        target = (o + d) % outer * inner
        scal = jnp.concatenate(
            [jnp.stack([here * y_local]), sketch_seeds,
             jnp.stack([target + (inner - 1 - y), target + y])]
        ).astype(i32)
        sent, kept = sketch_pair(field, scal, chunk)
        if inner == 2:
            kept = kept + neighbour(sent)
        part = shift(kept, d) if d else kept
        own = part if own is None else own + part
    chunks = [None] * count
    for d in order:
        came = shift(own, d) if d else own
        chunks[d * inner] = came
        if inner == 2:
            chunks[d * inner + 1] = neighbour(came)
    rows = jnp.concatenate(chunks, axis=0)
    gram = lax.dot_general(
        rows, rows, (((0,), (0,)), ((), ())), precision=lax.Precision.HIGHEST,
        preferred_element_type=f32,
    )
    gram = gram + other_core(gram)
    inverse = inverse_factor(gram)
    basis = lax.dot_general(
        rows, inverse, (((1,), (1,)), ((), ())), precision=lax.Precision.HIGHEST,
        preferred_element_type=f32,
    )
    basis = basis.reshape(outer, inner, chunk, RANK)
    basis = jnp.where(y == 1, basis[:, ::-1], basis)
    basis = jnp.roll(basis[::-1], o + 1, axis=0).reshape(x_local, RANK)
    basis_half = basis.astype(bf16)
    flat = field.reshape(x_local, y_local * z_local)
    owned = RANK // lax.axis_size("gx")
    c = lax.axis_index("gx")

    def product(index):
        part = lax.dynamic_slice_in_dim(basis_half, index * owned, owned, 1)
        return lax.dot_general(part, flat, (((0,), (0,)), ((), ())), preferred_element_type=f32)

    core = other_core(product(1 - c)) + product(c)
    return (basis, core.reshape(owned, y_local, z_local).astype(bf16))


def solution(mesh):
    in_specs = (P(("grp", "gx"), "yz", None), P("grp"))
    out_specs = (P(("grp", "gx"), None), P(("grp", "gx"), "yz", None))
    return jax.shard_map(local, mesh=mesh, in_specs=in_specs, out_specs=out_specs, check_vma=False)
```

```python
import jax
import jax.numpy as jnp
from jax import lax
from jax.experimental import pallas as pl
from jax.experimental.pallas import tpu as pltpu
from jax.sharding import PartitionSpec as P

RANK = 256
prime = 32749
f32, bf16, i32 = jnp.float32, jnp.bfloat16, jnp.int32


def remainder(value):
    quotient = (value.astype(f32) * (1.0 / prime)).astype(i32)
    rest = value - quotient * prime
    rest = jnp.where(rest < 0, rest + prime, rest)
    return jnp.where(rest >= prime, rest - prime, rest)


def omega_table(a, b, c, start, count):
    place = start + 1 + lax.broadcasted_iota(i32, (count, 1), 0)
    column = 1 + lax.broadcasted_iota(i32, (1, RANK), 1)
    first = remainder(a * place)
    second = remainder(b * column + c)
    square = remainder(place * place)
    third = remainder(c * column)
    mixed = remainder(remainder(first * second) + remainder(square * third))
    return mixed.astype(f32) * (2.0 / prime) - 1.0


LIMIT = 32 << 20
VMEM_SPACE = pl.BlockSpec(memory_space=pltpu.VMEM)
SMEM_SPACE = pl.BlockSpec(memory_space=pltpu.SMEM)
ANY_SPACE = pl.BlockSpec(memory_space=pl.ANY)
SUB = 64


def held(shape, dtype):
    return pltpu.VMEM(shape, dtype)


def call(kernel, name, out_shape, in_specs, flops=0, moved=0, **more):
    return pl.pallas_call(
        kernel,
        out_shape=out_shape,
        in_specs=in_specs,
        compiler_params=pltpu.CompilerParams(vmem_limit_bytes=LIMIT),
        cost_estimate=pl.CostEstimate(flops=flops, bytes_accessed=moved, transcendentals=0),
        name=name,
        **more,
    )


def sketch_chunks(field, here, seeds, wanted, sizes, joined, tables=None):
    outer, inner, chunk = sizes
    _, y_local, z_local = field.shape
    sub = min(SUB, chunk)
    stride = y_local + 1
    parts = chunk // sub
    total = len(wanted) * chunk

    def kernel(here_ref, seeds_ref, field_ref, *refs):
        refs = list(refs)
        if tables is not None:
            omega_z, omega_y = refs.pop(0), refs.pop(0)
        outs = [refs.pop(0) for _ in range(1 if joined else len(wanted))]
        flat = refs.pop(0)
        if tables is None:
            omega_z, omega_y = refs.pop(0), refs.pop(0)
        rows, first, second, sems = refs
        me = here_ref[0]
        o, y = me // inner, me % inner
        copies = []
        for k, (d, flip) in enumerate(wanted):
            chosen = lax.rem(o + d, outer) * inner + (inner - 1 - y if flip else y)
            copy = pltpu.make_async_copy(
                field_ref.at[pl.ds(chosen * chunk, chunk)], rows.at[pl.ds(k * chunk, chunk)], sems.at[k]
            )
            copy.start()
            copies.append(copy)
        if tables is None:
            omega_z[...] = omega_table(
                seeds_ref[3], seeds_ref[4], seeds_ref[5], 0, z_local
            ).astype(bf16)
            omega_y[...] = omega_table(
                seeds_ref[0], seeds_ref[1], seeds_ref[2], me * y_local, y_local
            )
        table_z = omega_z[...]
        scratch = (first, second)

        def spread(block):
            if block % parts == 0:
                copies[block // parts].wait()
            for x in range(sub):
                scratch[block % 2][x * stride:x * stride + y_local, :] = rows[block * sub + x].astype(f32)

        spread(0)
        for block in range(len(wanted) * parts):
            if block + 1 < len(wanted) * parts:
                spread(block + 1)
            low = block * sub
            sums = None
            for y_cell in range(y_local):
                cells = scratch[block % 2][pl.ds(y_cell, sub, stride=stride), :].astype(bf16)
                flat[low:low + sub, y_cell * z_local:(y_cell + 1) * z_local] = cells
                part = jnp.dot(cells, table_z, preferred_element_type=f32)
                part = part * omega_y[y_cell:y_cell + 1, :]
                sums = part if sums is None else sums + part
            if joined:
                outs[0][low:low + sub, :] = sums
            else:
                start = block % parts * sub
                outs[block // parts][start:start + sub, :] = sums

    count = 1 if joined else len(wanted)
    shape = jax.ShapeDtypeStruct((total if joined else chunk, RANK), f32)
    out_shape = [shape] * count + [held((total, y_local * z_local), bf16)]
    operands, in_specs = [here, seeds, field], [SMEM_SPACE, SMEM_SPACE, ANY_SPACE]
    if tables is None:
        out_shape += [held((z_local, RANK), bf16), held((y_local, RANK), f32)]
    else:
        operands += list(tables)
        in_specs += [VMEM_SPACE] * 2
    scratch_shapes = [
        pltpu.VMEM((total, y_local, z_local), bf16),
        pltpu.VMEM((sub * stride, z_local), f32),
        pltpu.VMEM((sub * stride, z_local), f32),
        pltpu.SemaphoreType.DMA((len(wanted),)),
    ]
    result = call(
        kernel, "sketch", out_shape, in_specs,
        flops=2 * total * y_local * z_local * RANK, moved=2 * total * y_local * z_local,
        scratch_shapes=scratch_shapes,
    )(*operands)
    tail = result[count + 1:] if tables is None else tables
    return result[:count], result[count], tail


def split3(value):
    high = value.astype(bf16)
    rest = value - high.astype(f32)
    middle = rest.astype(bf16)
    return high, middle, (rest - middle.astype(f32)).astype(bf16)


PANEL = 32


def inverse_factor_kernel(gram, out, state):
    size = gram.shape[0]
    state[...] = gram[...]
    lane = lax.broadcasted_iota(i32, (PANEL, 128), 1)
    row = lax.broadcasted_iota(i32, (PANEL, 128), 0)
    for low in range(0, size, PANEL):
        high = low + PANEL
        tile, offset = low // 128, low % 128
        rows = [state[low:high, 0:128], state[low:high, 128:256]]
        rows.append(jnp.where(lane == row + offset, 1.0, 0.0).astype(f32))
        done = [[None] * PANEL for _ in rows]
        for i in range(0, PANEL, 2):
            first = jnp.broadcast_to(rows[tile][:, offset + i:offset + i + 1], (PANEL, 128))
            second = jnp.broadcast_to(rows[tile][:, offset + i + 1:offset + i + 2], (PANEL, 128))
            d11, d12, d22 = first[i:i + 1], second[i:i + 1], second[i + 1:i + 2]
            scale = 1.0 / (d11 * d22 - d12 * d12)
            k11, k12, k22 = d22 * scale, d12 * scale, d11 * scale
            first = jnp.where(row > i + 1, first, 0.0)
            second = jnp.where(row > i + 1, second, 0.0)
            ratio = d12 / d11
            root1, root2 = lax.rsqrt(d11), lax.rsqrt(d22 - ratio * d12)
            for k in range(3):
                upper, lower = rows[k][i:i + 1], rows[k][i + 1:i + 2]
                done[k][i] = upper * root1
                done[k][i + 1] = (lower - ratio * upper) * root2
                if i + 2 < PANEL:
                    rows[k] = rows[k] - (
                        first * (k11 * upper - k12 * lower) + second * (k22 * lower - k12 * upper)
                    )
        factor = [jnp.concatenate(part, axis=0) for part in done]
        inside = (lane >= offset) & (lane < offset + PANEL)
        mixed = list(factor[:2])
        mixed[tile] = jnp.where(inside, factor[2], factor[tile])
        for k in range(2):
            if k < tile:
                value = mixed[k]
            elif k == tile:
                value = jnp.where(lane < offset + PANEL, mixed[k], 0.0)
            else:
                value = jnp.zeros((PANEL, 128), f32)
            out[low:high, 128 * k:128 * (k + 1)] = value
        if high < size:
            h, m, l = split3(jnp.concatenate(factor[:2], axis=1))
            eh, em, el = split3(jnp.concatenate(mixed, axis=1))
            left = jnp.concatenate([h, h, m, m, h, l], axis=0)
            right = jnp.concatenate([eh, em, eh, em, el, eh], axis=0)
            update = lax.dot_general(
                left, right, (((0,), (0,)), ((), ())), preferred_element_type=f32
            )
            lanes = lax.broadcasted_iota(i32, (size - high, size), 1)
            rest = jnp.where((lanes >= low) & (lanes < high), 0.0, state[high:, :])
            state[high:, :] = rest - update[high:, :]


def inverse_factor(gram):
    return call(
        inverse_factor_kernel, "inverse_factor", held(gram.shape, f32), [VMEM_SPACE],
        flops=3 * gram.shape[0] ** 3, moved=8 * gram.shape[0] ** 2,
        scratch_shapes=[pltpu.VMEM(gram.shape, f32)],
    )(gram)


def split2(value):
    high = value.astype(bf16)
    return high, (value - high.astype(f32)).astype(bf16)


def solve_rows(rows, inverse, here, core_index, sizes, places):
    outer, inner, chunk = sizes
    total = rows.shape[0]
    half = RANK // 2

    def kernel(here_ref, core_ref, rows_ref, inverse_ref, basis, turned, rounded):
        me = here_ref[0]
        o, y = me // inner, me % inner
        high, low = split2(inverse_ref[...])
        right = jnp.concatenate([high, high, low], axis=1)
        for k in range(outer * inner):
            d, flip = k // inner, k % inner
            high, low = split2(rows_ref[k * chunk:(k + 1) * chunk, :])
            left = jnp.concatenate([high, low, high], axis=1)
            value = lax.dot_general(left, right, (((1,), (1,)), ((), ())), preferred_element_type=f32)
            chosen = lax.rem(o + outer - d, outer) * inner + (inner - 1 - y if flip else y)
            basis[pl.ds(pl.multiple_of(chosen * chunk, chunk), chunk), :] = value
            rounded[places[k] * chunk:(places[k] + 1) * chunk, :] = value
        step = 128
        for start in range(0, total, step):
            block = rounded[start:start + step, :].T.astype(bf16)
            first = core_ref[0] == 0
            turned[:half, start:start + step] = jnp.where(first, block[half:], block[:half])
            turned[half:, start:start + step] = jnp.where(first, block[:half], block[half:])

    return call(
        kernel, "solve", [jax.ShapeDtypeStruct(rows.shape, f32), held((RANK, total), bf16)],
        [SMEM_SPACE, SMEM_SPACE, VMEM_SPACE, VMEM_SPACE],
        flops=6 * total * RANK ** 2, moved=8 * total * RANK,
        scratch_shapes=[pltpu.VMEM(rows.shape, f32)],
    )(here, core_index, rows, inverse)


WIDTH = 256


def product(turned, flats, low, high):
    half = RANK // 2

    def kernel(turned_ref, *refs):
        flat_refs, (other, own) = refs[:-2], refs[-2:]
        for start in range(low, high, WIDTH):
            sums, depth = None, 0
            for flat in flat_refs:
                part = jnp.dot(
                    turned_ref[:, depth:depth + flat.shape[0]], flat[:, start:start + WIDTH],
                    preferred_element_type=f32,
                )
                depth += flat.shape[0]
                sums = part if sums is None else sums + part
            other[:, start - low:start - low + WIDTH] = sums[:half]
            own[:, start - low:start - low + WIDTH] = sums[half:]

    shape = (half, high - low)
    depth = turned.shape[1]
    return call(
        kernel, "core", [held(shape, f32), held(shape, f32)], [VMEM_SPACE] * (1 + len(flats)),
        flops=2 * RANK * depth * (high - low), moved=2 * depth * (high - low),
    )(turned, *flats)


def finish(own, came, y_local, z_local):
    half = own[0].shape[0]
    pieces = len(own)
    cells = y_local // pieces
    stride = y_local + 1
    step = min(half, 32)

    def kernel(*refs):
        out, scratch, sems = refs[-3:]
        rounded = scratch[1]
        spread = scratch[0]
        copies = []
        for start in range(0, half, step):
            for y_cell in range(y_local):
                k, at = y_cell // cells, y_cell % cells * z_local
                spread[pl.ds(start * stride + y_cell, step, stride=stride), :] = (
                    refs[k][start:start + step, at:at + z_local]
                    + refs[pieces + k][start:start + step, at:at + z_local]
                )
            for r in range(start, start + step):
                rounded[r] = spread[r * stride:r * stride + y_local, :].astype(bf16)
            copy = pltpu.make_async_copy(
                rounded.at[pl.ds(start, step)], out.at[pl.ds(start, step)], sems.at[start // step]
            )
            copy.start()
            copies.append(copy)
        for copy in copies:
            copy.wait()

    return call(
        lambda *refs: kernel(*refs[:-3], (refs[-3], refs[-2]), refs[-1]),
        "finish", jax.ShapeDtypeStruct((half, y_local, z_local), bf16), [VMEM_SPACE] * (2 * pieces),
        out_specs=ANY_SPACE, moved=10 * half * y_local * z_local,
        scratch_shapes=[
            pltpu.VMEM((half * stride, z_local), f32), pltpu.VMEM((half, y_local, z_local), bf16),
            pltpu.SemaphoreType.DMA((half // step,)),
        ],
    )(*own, *came)


def local(field, sketch_seeds):
    x_local, y_local, z_local = field.shape
    count = lax.axis_size("yz")
    inner = 2 if count % 2 == 0 else 1
    outer = count // inner
    chunk = x_local // count
    here = lax.axis_index("yz")
    o, y = here // inner, here % inner

    def neighbour(value):
        return lax.ppermute(value, "yz", [(i, i ^ 1) for i in range(count)])

    def shift(value, d):
        pairs = [(i, (i // inner + d) % outer * inner + i % inner) for i in range(count)]
        return lax.ppermute(value, "yz", pairs)

    def other_core(value):
        return lax.ppermute(value, "gx", [(0, 1), (1, 0)])

    sizes = (outer, inner, chunk)
    place = here.reshape(1).astype(i32)
    core_index = lax.axis_index("gx").reshape(1).astype(i32)
    order = list(range(1, outer)) + [0]
    cut = (outer + 1) // 2
    groups = [group for group in (order[:cut], order[cut:]) if group]
    wanted, flats, sends, tables = [], [], [], None
    if inner == 2:
        for group in groups:
            pairs = [(d, 1) for d in group]
            (rows,), flat, tables = sketch_chunks(
                field, place, sketch_seeds, pairs, sizes, True, tables
            )
            sends.append(neighbour(rows))
            wanted += pairs
            flats.append(flat)
    pairs = [(d, 0) for d in order]
    kept, flat, tables = sketch_chunks(field, place, sketch_seeds, pairs, sizes, False, tables)
    wanted += pairs
    flats.append(flat)
    own = None
    for k, d in enumerate(order):
        part = kept[k]
        if inner == 2:
            came = sends[0] if k < cut else sends[1]
            at = (k if k < cut else k - cut) * chunk
            part = part + came[at:at + chunk]
        part = shift(part, d) if d else part
        own = part if own is None else own + part
    chunks = [None] * count
    for d in order:
        came = shift(own, d) if d else own
        chunks[d * inner] = came
        if inner == 2:
            chunks[d * inner + 1] = neighbour(came)
    rows = jnp.concatenate(chunks, axis=0)
    gram = lax.dot_general(
        rows, rows, (((0,), (0,)), ((), ())), precision=lax.Precision.HIGHEST,
        preferred_element_type=f32,
    )
    gram = gram + other_core(gram)
    inverse = inverse_factor(gram)
    places = [wanted.index(((outer - k // inner) % outer, k % inner)) for k in range(count)]
    basis, turned = solve_rows(rows, inverse, place, core_index, sizes, places)
    columns = y_local * z_local
    pieces = 2
    own_parts, came_parts = [], []
    for k in range(pieces):
        other, mine = product(turned, flats, columns * k // pieces, columns * (k + 1) // pieces)
        came_parts.append(other_core(other))
        own_parts.append(mine)
    core = finish(own_parts, came_parts, y_local, z_local)
    return (basis, core)


def solution(mesh):
    in_specs = (P(("grp", "gx"), "yz", None), P("grp"))
    out_specs = (P(("grp", "gx"), None), P(("grp", "gx"), "yz", None))
    return jax.shard_map(local, mesh=mesh, in_specs=in_specs, out_specs=out_specs, check_vma=False)
```

```python
import jax
import jax.numpy as jnp
from jax import lax
from jax.experimental import pallas as pl
from jax.experimental.pallas import tpu as pltpu
from jax.sharding import PartitionSpec as P

RANK = 256
prime = 32749
f32, bf16, i32 = jnp.float32, jnp.bfloat16, jnp.int32


def remainder(value):
    quotient = (value.astype(f32) * (1.0 / prime)).astype(i32)
    rest = value - quotient * prime
    rest = jnp.where(rest < 0, rest + prime, rest)
    return jnp.where(rest >= prime, rest - prime, rest)


def omega_table(a, b, c, start, count):
    place = start + 1 + lax.broadcasted_iota(i32, (count, 1), 0)
    column = 1 + lax.broadcasted_iota(i32, (1, RANK), 1)
    first = remainder(a * place)
    second = remainder(b * column + c)
    square = remainder(place * place)
    third = remainder(c * column)
    mixed = remainder(remainder(first * second) + remainder(square * third))
    return mixed.astype(f32) * (2.0 / prime) - 1.0


LIMIT = 14 << 20
VMEM_SPACE = pl.BlockSpec(memory_space=pltpu.VMEM)
SMEM_SPACE = pl.BlockSpec(memory_space=pltpu.SMEM)
ANY_SPACE = pl.BlockSpec(memory_space=pl.ANY)
HBM_SPACE = pl.BlockSpec(memory_space=pltpu.HBM)
SUB = 64


def held(shape, dtype):
    return pltpu.VMEM(shape, dtype)


def call(kernel, out_shape, in_specs, flops=0, moved=0, **more):
    return pl.pallas_call(
        kernel,
        out_shape=out_shape,
        in_specs=in_specs,
        compiler_params=pltpu.CompilerParams(vmem_limit_bytes=LIMIT),
        cost_estimate=pl.CostEstimate(flops=flops, bytes_accessed=moved, transcendentals=0),
        **more,
    )


def sketch_chunks(field, seeds, wanted, sizes, joined, tables=None):
    outer, inner, chunk = sizes
    _, y_local, z_local = field.shape
    sub = min(SUB, chunk)
    stride = y_local + 1
    parts = chunk // sub
    total = len(wanted) * chunk

    def kernel(seeds_ref, field_ref, *refs):
        refs = list(refs)
        if tables is not None:
            omega_z, omega_y = refs.pop(0), refs.pop(0)
        outs = [refs.pop(0) for _ in range(1 if joined else len(wanted))]
        flat = refs.pop(0)
        if tables is None:
            omega_z, omega_y = refs.pop(0), refs.pop(0)
        rows, first, second, sems = refs
        me = lax.axis_index("yz")
        o, y = me // inner, me % inner
        copies = []
        for k, (d, flip) in enumerate(wanted):
            chosen = lax.rem(o + d, outer) * inner + (inner - 1 - y if flip else y)
            copy = pltpu.make_async_copy(
                field_ref.at[pl.ds(chosen * chunk, chunk)], rows.at[pl.ds(k * chunk, chunk)], sems.at[k]
            )
            copy.start()
            copies.append(copy)
        if tables is None:
            omega_z[...] = omega_table(
                seeds_ref[3], seeds_ref[4], seeds_ref[5], 0, z_local
            ).astype(bf16)
            omega_y[...] = omega_table(
                seeds_ref[0], seeds_ref[1], seeds_ref[2], me * y_local, y_local
            )
        table_z = omega_z[...]
        scratch = (first, second)

        def spread(block):
            if block % parts == 0:
                copies[block // parts].wait()
            for x in range(sub):
                scratch[block % 2][x * stride:x * stride + y_local, :] = rows[block * sub + x].astype(f32)

        spread(0)
        for block in range(len(wanted) * parts):
            if block + 1 < len(wanted) * parts:
                spread(block + 1)
            low = block * sub
            sums = None
            for y_cell in range(y_local):
                cells = scratch[block % 2][pl.ds(y_cell, sub, stride=stride), :].astype(bf16)
                flat[low:low + sub, y_cell * z_local:(y_cell + 1) * z_local] = cells
                part = jnp.dot(cells, table_z, preferred_element_type=f32)
                part = part * omega_y[y_cell:y_cell + 1, :]
                sums = part if sums is None else sums + part
            if joined:
                outs[0][low:low + sub, :] = sums
            else:
                start = block % parts * sub
                outs[block // parts][start:start + sub, :] = sums

    count = 1 if joined else len(wanted)
    shape = jax.ShapeDtypeStruct((total if joined else chunk, RANK), f32)
    out_shape = [shape] * count + [held((total, y_local * z_local), bf16)]
    operands = [seeds, pltpu.with_memory_space_constraint(field, pltpu.HBM)]
    in_specs = [SMEM_SPACE, HBM_SPACE]
    if tables is None:
        out_shape += [held((z_local, RANK), bf16), held((y_local, RANK), f32)]
    else:
        operands += list(tables)
        in_specs += [VMEM_SPACE] * 2
    scratch_shapes = [
        pltpu.VMEM((total, y_local, z_local), bf16),
        pltpu.VMEM((sub * stride, z_local), f32),
        pltpu.VMEM((sub * stride, z_local), f32),
        pltpu.SemaphoreType.DMA((len(wanted),)),
    ]
    result = call(
        kernel, out_shape, in_specs,
        flops=2 * total * y_local * z_local * RANK, moved=2 * total * y_local * z_local,
        scratch_shapes=scratch_shapes,
    )(*operands)
    tail = result[count + 1:] if tables is None else tables
    return result[:count], result[count], tail


def split3(value):
    high = value.astype(bf16)
    rest = value - high.astype(f32)
    middle = rest.astype(bf16)
    return high, middle, (rest - middle.astype(f32)).astype(bf16)


PANEL = 32


def inverse_factor_kernel(gram, came, out, state):
    size = gram.shape[0]
    state[...] = gram[...] + came[...]
    lane = lax.broadcasted_iota(i32, (PANEL, 128), 1)
    row = lax.broadcasted_iota(i32, (PANEL, 128), 0)
    for low in range(0, size, PANEL):
        high = low + PANEL
        tile, offset = low // 128, low % 128
        rows = [state[low:high, 0:128], state[low:high, 128:256]]
        rows.append(jnp.where(lane == row + offset, 1.0, 0.0).astype(f32))
        done = [[None] * PANEL for _ in rows]
        for i in range(0, PANEL, 2):
            first = jnp.broadcast_to(rows[tile][:, offset + i:offset + i + 1], (PANEL, 128))
            second = jnp.broadcast_to(rows[tile][:, offset + i + 1:offset + i + 2], (PANEL, 128))
            d11, d12, d22 = first[i:i + 1], second[i:i + 1], second[i + 1:i + 2]
            scale = 1.0 / (d11 * d22 - d12 * d12)
            k11, k12, k22 = d22 * scale, d12 * scale, d11 * scale
            first = jnp.where(row > i + 1, first, 0.0)
            second = jnp.where(row > i + 1, second, 0.0)
            ratio = d12 / d11
            root1, root2 = lax.rsqrt(d11), lax.rsqrt(d22 - ratio * d12)
            for k in range(3):
                upper, lower = rows[k][i:i + 1], rows[k][i + 1:i + 2]
                done[k][i] = upper * root1
                done[k][i + 1] = (lower - ratio * upper) * root2
                if i + 2 < PANEL:
                    rows[k] = rows[k] - (
                        first * (k11 * upper - k12 * lower) + second * (k22 * lower - k12 * upper)
                    )
        factor = [jnp.concatenate(part, axis=0) for part in done]
        inside = (lane >= offset) & (lane < offset + PANEL)
        mixed = list(factor[:2])
        mixed[tile] = jnp.where(inside, factor[2], factor[tile])
        for k in range(2):
            if k < tile:
                value = mixed[k]
            elif k == tile:
                value = jnp.where(lane < offset + PANEL, mixed[k], 0.0)
            else:
                value = jnp.zeros((PANEL, 128), f32)
            out[low:high, 128 * k:128 * (k + 1)] = value
        if high < size:
            h, m, l = split3(jnp.concatenate(factor[:2], axis=1))
            eh, em, el = split3(jnp.concatenate(mixed, axis=1))
            left = jnp.concatenate([h, h, m, m, h, l], axis=0)
            right = jnp.concatenate([eh, em, eh, em, el, eh], axis=0)
            update = lax.dot_general(
                left, right, (((0,), (0,)), ((), ())), preferred_element_type=f32
            )
            lanes = lax.broadcasted_iota(i32, (size - high, size), 1)
            rest = jnp.where((lanes >= low) & (lanes < high), 0.0, state[high:, :])
            state[high:, :] = rest - update[high:, :]


def inverse_factor(gram, came):
    return call(
        inverse_factor_kernel, held(gram.shape, f32), [VMEM_SPACE] * 2,
        flops=3 * gram.shape[0] ** 3, moved=8 * gram.shape[0] ** 2,
        scratch_shapes=[pltpu.VMEM(gram.shape, f32)],
    )(gram, came)


def merge(kept, came):
    chunk = kept[0].shape[0]

    def kernel(*refs):
        came_ref = refs[len(kept)]
        for k in range(len(kept)):
            refs[len(kept) + 1 + k][...] = refs[k][...] + came_ref[k * chunk:(k + 1) * chunk, :]

    return call(
        kernel, [held(kept[0].shape, f32)] * len(kept), [VMEM_SPACE] * (len(kept) + 1),
        flops=came.size, moved=12 * came.size,
    )(*kept, came)


def total_of(parts):
    def kernel(*refs):
        sums = refs[0][...]
        for ref in refs[1:-1]:
            sums = sums + ref[...]
        refs[-1][...] = sums

    return call(
        kernel, held(parts[0].shape, f32), [VMEM_SPACE] * len(parts),
        flops=parts[0].size * len(parts), moved=4 * parts[0].size * len(parts),
    )(*parts)


def gram_of(chunks):
    chunk = chunks[0].shape[0]
    total = len(chunks) * chunk

    def kernel(*refs):
        rows_refs, (out, terms) = refs[:-2], refs[-2:]
        for k, ref in enumerate(rows_refs):
            for j, term in enumerate(split3(ref[...])):
                terms[k * chunk:(k + 1) * chunk, j * RANK:(j + 1) * RANK] = term
        over_rows = (((0,), (0,)), ((), ()))
        first = lax.dot_general(
            terms[:, :RANK], terms[...], over_rows, preferred_element_type=f32
        )
        middle = terms[:, RANK:2 * RANK]
        second = lax.dot_general(middle, middle, over_rows, preferred_element_type=f32)
        mixed = first[:, RANK:2 * RANK] + first[:, 2 * RANK:]
        out[...] = first[:, :RANK] + (second + (mixed + mixed.T))

    return call(
        kernel, held((RANK, RANK), f32), [VMEM_SPACE] * len(chunks),
        flops=8 * total * RANK ** 2, moved=4 * total * RANK,
        scratch_shapes=[pltpu.VMEM((total, 3 * RANK), bf16)],
    )(*chunks)


def split2(value):
    high = value.astype(bf16)
    return high, (value - high.astype(f32)).astype(bf16)


def solve_rows(chunks, inverse, sizes, places):
    outer, inner, chunk = sizes
    total = len(chunks) * chunk
    half = RANK // 2

    def kernel(inverse_ref, *refs):
        rows_refs, (basis, turned, rounded) = refs[:-3], refs[-3:]
        me = lax.axis_index("yz")
        o, y = me // inner, me % inner
        high, low = split2(inverse_ref[...])
        right = jnp.concatenate([high, high, low], axis=1)
        for k in range(outer * inner):
            d, flip = k // inner, k % inner
            high, low = split2(rows_refs[k][...])
            left = jnp.concatenate([high, low, high], axis=1)
            value = lax.dot_general(left, right, (((1,), (1,)), ((), ())), preferred_element_type=f32)
            chosen = lax.rem(o + outer - d, outer) * inner + (inner - 1 - y if flip else y)
            basis[pl.ds(pl.multiple_of(chosen * chunk, chunk), chunk), :] = value
            rounded[places[k] * chunk:(places[k] + 1) * chunk, :] = value
        step = 128
        for start in range(0, total, step):
            block = rounded[start:start + step, :].T.astype(bf16)
            first = lax.axis_index("gx") == 0
            turned[:half, start:start + step] = jnp.where(first, block[half:], block[:half])
            turned[half:, start:start + step] = jnp.where(first, block[:half], block[half:])

    return call(
        kernel, [jax.ShapeDtypeStruct((total, RANK), f32), held((RANK, total), bf16)],
        [VMEM_SPACE] * (1 + len(chunks)),
        flops=6 * total * RANK ** 2, moved=8 * total * RANK,
        scratch_shapes=[pltpu.VMEM((total, RANK), f32)],
    )(inverse, *chunks)


WIDTH = 256


def product(turned, flats, low, high):
    half = RANK // 2

    def kernel(turned_ref, *refs):
        flat_refs, (other, own) = refs[:-2], refs[-2:]
        for start in range(low, high, WIDTH):
            sums, depth = None, 0
            for flat in flat_refs:
                part = jnp.dot(
                    turned_ref[:, depth:depth + flat.shape[0]], flat[:, start:start + WIDTH],
                    preferred_element_type=f32,
                )
                depth += flat.shape[0]
                sums = part if sums is None else sums + part
            other[:, start - low:start - low + WIDTH] = sums[:half]
            own[:, start - low:start - low + WIDTH] = sums[half:]

    shape = (half, high - low)
    depth = turned.shape[1]
    return call(
        kernel, [held(shape, f32), held(shape, f32)], [VMEM_SPACE] * (1 + len(flats)),
        flops=2 * RANK * depth * (high - low), moved=2 * depth * (high - low),
    )(turned, *flats)


def finish(own, came, y_local, z_local):
    half = own[0].shape[0]
    pieces = len(own)
    cells = y_local // pieces
    stride = y_local + 1
    step = min(half, 32)

    def kernel(*refs):
        out, scratch, sems = refs[-3:]
        rounded = scratch[1]
        spread = scratch[0]
        copies = []
        for start in range(0, half, step):
            for y_cell in range(y_local):
                k, at = y_cell // cells, y_cell % cells * z_local
                spread[pl.ds(start * stride + y_cell, step, stride=stride), :] = (
                    refs[k][start:start + step, at:at + z_local]
                    + refs[pieces + k][start:start + step, at:at + z_local]
                )
            for r in range(start, start + step):
                rounded[r] = spread[r * stride:r * stride + y_local, :].astype(bf16)
            copy = pltpu.make_async_copy(
                rounded.at[pl.ds(start, step)], out.at[pl.ds(start, step)], sems.at[start // step]
            )
            copy.start()
            copies.append(copy)
        for copy in copies:
            copy.wait()

    return call(
        lambda *refs: kernel(*refs[:-3], (refs[-3], refs[-2]), refs[-1]),
        jax.ShapeDtypeStruct((half, y_local, z_local), bf16), [VMEM_SPACE] * (2 * pieces),
        out_specs=ANY_SPACE, moved=10 * half * y_local * z_local,
        scratch_shapes=[
            pltpu.VMEM((half * stride, z_local), f32), pltpu.VMEM((half, y_local, z_local), bf16),
            pltpu.SemaphoreType.DMA((half // step,)),
        ],
    )(*own, *came)


def local(field, sketch_seeds):
    x_local, y_local, z_local = field.shape
    count = lax.axis_size("yz")
    inner = 2 if count % 2 == 0 else 1
    outer = count // inner
    chunk = x_local // count

    def neighbour(value):
        return lax.ppermute(value, "yz", [(i, i ^ 1) for i in range(count)])

    def shift(value, d):
        pairs = [(i, (i // inner + d) % outer * inner + i % inner) for i in range(count)]
        return lax.ppermute(value, "yz", pairs)

    def other_core(value):
        return lax.ppermute(value, "gx", [(0, 1), (1, 0)])

    sizes = (outer, inner, chunk)
    order = sorted(range(1, outer), key=lambda d: -min(d, outer - d)) + [0]
    cut = (outer + 1) // 2
    groups = [group for group in (order[:cut], order[cut:]) if group]
    wanted, flats, sends, tables = [], [], [], None
    if inner == 2:
        for group in groups:
            pairs = [(d, 1) for d in group]
            (rows,), flat, tables = sketch_chunks(field, sketch_seeds, pairs, sizes, True, tables)
            sends.append(neighbour(rows))
            wanted += pairs
            flats.append(flat)
    parts = []
    for k, group in enumerate(groups):
        pairs = [(d, 0) for d in group]
        kept, flat, tables = sketch_chunks(
            field, sketch_seeds, pairs, sizes, False, tables
        )
        wanted += pairs
        flats.append(flat)
        if inner == 2:
            kept = merge(kept, sends[k])
        for j, d in enumerate(group):
            parts.append(shift(kept[j], d) if d else kept[j])
    own = total_of(parts)
    chunks = [None] * count
    near = [0] + sorted(range(1, outer), key=lambda d: min(d, outer - d))
    for d in near:
        came = shift(own, d) if d else own
        chunks[d * inner] = came
        if inner == 2:
            chunks[d * inner + 1] = neighbour(came)
    gram = gram_of(chunks)
    came = other_core(gram)
    inverse = inverse_factor(gram, came)
    places = [wanted.index(((outer - k // inner) % outer, k % inner)) for k in range(count)]
    basis, turned = solve_rows(chunks, inverse, sizes, places)
    columns = y_local * z_local
    own_parts, came_parts = [], []
    for k in range(PIECES):
        other, mine = product(
            turned, flats, columns * k // PIECES, columns * (k + 1) // PIECES
        )
        came_parts.append(other_core(other))
        own_parts.append(mine)
    core = finish(own_parts, came_parts, y_local, z_local)
    return (basis, core)


PIECES = 2


def solution(mesh):
    in_specs = (P(("grp", "gx"), "yz", None), P("grp"))
    out_specs = (P(("grp", "gx"), None), P(("grp", "gx"), "yz", None))

    return jax.shard_map(local, mesh=mesh, in_specs=in_specs, out_specs=out_specs, check_vma=False)
```

```python
import jax
import jax.numpy as jnp
from jax import lax
from jax.experimental import pallas as pl
from jax.experimental.pallas import tpu as pltpu
from jax.sharding import PartitionSpec as P

RANK = 256
prime = 32749
f32, bf16, i32 = jnp.float32, jnp.bfloat16, jnp.int32


def remainder(value):
    quotient = (value.astype(f32) * (1.0 / prime)).astype(i32)
    rest = value - quotient * prime
    rest = jnp.where(rest < 0, rest + prime, rest)
    return jnp.where(rest >= prime, rest - prime, rest)


def omega_table(a, b, c, start, count):
    place = start + 1 + lax.broadcasted_iota(i32, (count, 1), 0)
    column = 1 + lax.broadcasted_iota(i32, (1, RANK), 1)
    first = remainder(a * place)
    second = remainder(b * column + c)
    square = remainder(place * place)
    third = remainder(c * column)
    mixed = remainder(remainder(first * second) + remainder(square * third))
    return mixed.astype(f32) * (2.0 / prime) - 1.0


LIMIT = 14 << 20
VMEM_SPACE = pl.BlockSpec(memory_space=pltpu.VMEM)
SMEM_SPACE = pl.BlockSpec(memory_space=pltpu.SMEM)
ANY_SPACE = pl.BlockSpec(memory_space=pl.ANY)
HBM_SPACE = pl.BlockSpec(memory_space=pltpu.HBM)
SUB = 64


def held(shape, dtype):
    return pltpu.VMEM(shape, dtype)


def call(kernel, out_shape, in_specs, flops=0, moved=0, **more):
    return pl.pallas_call(
        kernel,
        out_shape=out_shape,
        in_specs=in_specs,
        compiler_params=pltpu.CompilerParams(vmem_limit_bytes=LIMIT),
        cost_estimate=pl.CostEstimate(flops=flops, bytes_accessed=moved, transcendentals=0),
        **more,
    )


CELLS = 4


def sketch_chunks(source, seeds, wanted, first, span, sizes, joined, tables=None):
    outer, inner, chunk = sizes
    x_local, y_local, z_local = source.shape
    sub = min(SUB, chunk)
    stride = y_local + 1
    parts = chunk // sub
    total = span * chunk
    opening = tables is None

    def kernel(*refs):
        refs = list(refs)
        seeds_ref = refs.pop(0) if opening else None
        source_ref = refs.pop(0)
        if not opening:
            omega_z, omega_y = refs.pop(0), refs.pop(0)
        outs = [refs.pop(0) for _ in range(1 if joined else span)]
        flat = refs.pop(0)
        copies = []
        if opening:
            rows, omega_z, omega_y = refs.pop(0), refs.pop(0), refs.pop(0)
            sems = refs.pop()
            me = lax.axis_index("yz")
            o, y = me // inner, me % inner
            for k, (d, flip) in enumerate(wanted):
                chosen = lax.rem(o + d, outer) * inner + (inner - 1 - y if flip else y)
                copy = pltpu.make_async_copy(
                    source_ref.at[pl.ds(chosen * chunk, chunk)],
                    rows.at[pl.ds(k * chunk, chunk)],
                    sems.at[k],
                )
                copy.start()
                copies.append(copy)
            omega_z[...] = omega_table(
                seeds_ref[3], seeds_ref[4], seeds_ref[5], 0, z_local
            ).astype(bf16)
            omega_y[...] = omega_table(
                seeds_ref[0], seeds_ref[1], seeds_ref[2], me * y_local, y_local
            )
        else:
            rows = source_ref
        scratch = refs
        table_z = omega_z[...]

        def spread(block):
            if opening and block % parts == 0:
                copies[first + block // parts].wait()
            for x in range(sub):
                scratch[block % 2][x * stride:x * stride + y_local, :] = (
                    rows[first * chunk + block * sub + x].astype(f32)
                )

        spread(0)
        for block in range(span * parts):
            if block + 1 < span * parts:
                spread(block + 1)
            low = block * sub
            sums = None
            for y_cell in range(0, y_local, CELLS):
                cells = []
                for y_at in range(y_cell, y_cell + CELLS):
                    cell = scratch[block % 2][pl.ds(y_at, sub, stride=stride), :].astype(bf16)
                    flat[low:low + sub, y_at * z_local:(y_at + 1) * z_local] = cell
                    cells.append(cell)
                parted = jnp.dot(
                    jnp.concatenate(cells, axis=0), table_z, preferred_element_type=f32
                )
                for k in range(CELLS):
                    part = parted[k * sub:(k + 1) * sub] * omega_y[y_cell + k:y_cell + k + 1, :]
                    sums = part if sums is None else sums + part
            if joined:
                outs[0][low:low + sub, :] = sums
            else:
                start = block % parts * sub
                outs[block // parts][start:start + sub, :] = sums
        for k, copy in enumerate(copies):
            if not first <= k < first + span:
                copy.wait()

    count = 1 if joined else span
    shape = held((total if joined else chunk, RANK), f32)
    out_shape = [shape] * count + [held((total, y_local * z_local), bf16)]
    scratch_shapes = [pltpu.VMEM((sub * stride, z_local), f32)] * 2
    if opening:
        operands = [seeds, pltpu.with_memory_space_constraint(source, pltpu.HBM)]
        in_specs = [SMEM_SPACE, HBM_SPACE]
        out_shape += [
            held((x_local, y_local, z_local), bf16),
            held((z_local, RANK), bf16),
            held((y_local, RANK), f32),
        ]
        scratch_shapes = scratch_shapes + [pltpu.SemaphoreType.DMA((len(wanted),))]
    else:
        operands = [source] + list(tables)
        in_specs = [VMEM_SPACE] * 3
    result = call(
        kernel, out_shape, in_specs,
        flops=2 * total * y_local * z_local * RANK, moved=2 * total * y_local * z_local,
        scratch_shapes=scratch_shapes,
    )(*operands)
    if opening:
        source, tables = result[count + 1], result[count + 2:]
    return result[:count], result[count], source, tables


def split3(value):
    high = value.astype(bf16)
    rest = value - high.astype(f32)
    middle = rest.astype(bf16)
    return high, middle, (rest - middle.astype(f32)).astype(bf16)


PANEL = 32


def inverse_factor_kernel(gram, came, out, state):
    size = gram.shape[0]
    state[...] = gram[...] + came[...]
    lane = lax.broadcasted_iota(i32, (PANEL, 128), 1)
    row = lax.broadcasted_iota(i32, (PANEL, 128), 0)
    for low in range(0, size, PANEL):
        high = low + PANEL
        tile, offset = low // 128, low % 128
        rows = [state[low:high, 0:128], state[low:high, 128:256]]
        rows.append(jnp.where(lane == row + offset, 1.0, 0.0).astype(f32))
        done = [[None] * PANEL for _ in rows]
        for i in range(0, PANEL, 2):
            first = jnp.broadcast_to(rows[tile][:, offset + i:offset + i + 1], (PANEL, 128))
            second = jnp.broadcast_to(rows[tile][:, offset + i + 1:offset + i + 2], (PANEL, 128))
            d11, d12, d22 = first[i:i + 1], second[i:i + 1], second[i + 1:i + 2]
            scale = 1.0 / (d11 * d22 - d12 * d12)
            k11, k12, k22 = d22 * scale, d12 * scale, d11 * scale
            first = jnp.where(row > i + 1, first, 0.0)
            second = jnp.where(row > i + 1, second, 0.0)
            ratio = d12 / d11
            root1, root2 = lax.rsqrt(d11), lax.rsqrt(d22 - ratio * d12)
            for k in range(3):
                upper, lower = rows[k][i:i + 1], rows[k][i + 1:i + 2]
                done[k][i] = upper * root1
                done[k][i + 1] = (lower - ratio * upper) * root2
                if i + 2 < PANEL:
                    rows[k] = rows[k] - (
                        first * (k11 * upper - k12 * lower) + second * (k22 * lower - k12 * upper)
                    )
        factor = [jnp.concatenate(part, axis=0) for part in done]
        inside = (lane >= offset) & (lane < offset + PANEL)
        mixed = list(factor[:2])
        mixed[tile] = jnp.where(inside, factor[2], factor[tile])
        for k in range(2):
            if k < tile:
                value = mixed[k]
            elif k == tile:
                value = jnp.where(lane < offset + PANEL, mixed[k], 0.0)
            else:
                value = jnp.zeros((PANEL, 128), f32)
            out[low:high, 128 * k:128 * (k + 1)] = value
        if high < size:
            h, m, l = split3(jnp.concatenate(factor[:2], axis=1))
            eh, em, el = split3(jnp.concatenate(mixed, axis=1))
            left = jnp.concatenate([h, h, m, m, h, l], axis=0)
            right = jnp.concatenate([eh, em, eh, em, el, eh], axis=0)
            update = lax.dot_general(
                left, right, (((0,), (0,)), ((), ())), preferred_element_type=f32
            )
            lanes = lax.broadcasted_iota(i32, (size - high, size), 1)
            rest = jnp.where((lanes >= low) & (lanes < high), 0.0, state[high:, :])
            state[high:, :] = rest - update[high:, :]


def inverse_factor(gram, came):
    return call(
        inverse_factor_kernel, held(gram.shape, f32), [VMEM_SPACE] * 2,
        flops=3 * gram.shape[0] ** 3, moved=8 * gram.shape[0] ** 2,
        scratch_shapes=[pltpu.VMEM(gram.shape, f32)],
    )(gram, came)


def merge(kept, came):
    chunk = kept[0].shape[0]

    def kernel(*refs):
        came_ref = refs[len(kept)]
        for k in range(len(kept)):
            refs[len(kept) + 1 + k][...] = refs[k][...] + came_ref[k * chunk:(k + 1) * chunk, :]

    return call(
        kernel, [held(kept[0].shape, f32)] * len(kept), [VMEM_SPACE] * (len(kept) + 1),
        flops=came.size, moved=12 * came.size,
    )(*kept, came)


def total_of(parts):
    def kernel(*refs):
        sums = refs[0][...]
        for ref in refs[1:-1]:
            sums = sums + ref[...]
        refs[-1][...] = sums

    return call(
        kernel, held(parts[0].shape, f32), [VMEM_SPACE] * len(parts),
        flops=parts[0].size * len(parts), moved=4 * parts[0].size * len(parts),
    )(*parts)


def gram_of(chunks):
    chunk = chunks[0].shape[0]
    total = len(chunks) * chunk

    def kernel(*refs):
        rows_refs, (out, terms) = refs[:-2], refs[-2:]
        for k, ref in enumerate(rows_refs):
            for j, term in enumerate(split3(ref[...])):
                terms[k * chunk:(k + 1) * chunk, j * RANK:(j + 1) * RANK] = term
        over_rows = (((0,), (0,)), ((), ()))
        first = lax.dot_general(
            terms[:, :RANK], terms[...], over_rows, preferred_element_type=f32
        )
        middle = terms[:, RANK:2 * RANK]
        second = lax.dot_general(middle, middle, over_rows, preferred_element_type=f32)
        mixed = first[:, RANK:2 * RANK] + first[:, 2 * RANK:]
        out[...] = first[:, :RANK] + (second + (mixed + mixed.T))

    return call(
        kernel, held((RANK, RANK), f32), [VMEM_SPACE] * len(chunks),
        flops=8 * total * RANK ** 2, moved=4 * total * RANK,
        scratch_shapes=[pltpu.VMEM((total, 3 * RANK), bf16)],
    )(*chunks)


def split2(value):
    high = value.astype(bf16)
    return high, (value - high.astype(f32)).astype(bf16)


def solve_rows(chunks, inverse, sizes, places):
    outer, inner, chunk = sizes
    total = len(chunks) * chunk
    half = RANK // 2

    def kernel(inverse_ref, *refs):
        rows_refs, (basis, turned, rounded) = refs[:-3], refs[-3:]
        me = lax.axis_index("yz")
        o, y = me // inner, me % inner
        high, low = split2(inverse_ref[...])
        right = jnp.concatenate([high, high, low], axis=1)
        for k in range(outer * inner):
            d, flip = k // inner, k % inner
            high, low = split2(rows_refs[k][...])
            left = jnp.concatenate([high, low, high], axis=1)
            value = lax.dot_general(left, right, (((1,), (1,)), ((), ())), preferred_element_type=f32)
            chosen = lax.rem(o + outer - d, outer) * inner + (inner - 1 - y if flip else y)
            basis[pl.ds(pl.multiple_of(chosen * chunk, chunk), chunk), :] = value
            rounded[places[k] * chunk:(places[k] + 1) * chunk, :] = value
        step = 128
        for start in range(0, total, step):
            block = rounded[start:start + step, :].T.astype(bf16)
            first = lax.axis_index("gx") == 0
            turned[:half, start:start + step] = jnp.where(first, block[half:], block[:half])
            turned[half:, start:start + step] = jnp.where(first, block[:half], block[half:])

    return call(
        kernel, [held((total, RANK), f32), held((RANK, total), bf16)],
        [VMEM_SPACE] * (1 + len(chunks)),
        flops=6 * total * RANK ** 2, moved=8 * total * RANK,
        scratch_shapes=[pltpu.VMEM((total, RANK), f32)],
    )(inverse, *chunks)


WIDTH = 256


def product(turned, flats, low, high):
    half = RANK // 2

    def kernel(turned_ref, *refs):
        flat_refs, (other, own) = refs[:-2], refs[-2:]
        for start in range(low, high, WIDTH):
            sums, depth = None, 0
            for flat in flat_refs:
                part = jnp.dot(
                    turned_ref[:, depth:depth + flat.shape[0]], flat[:, start:start + WIDTH],
                    preferred_element_type=f32,
                )
                depth += flat.shape[0]
                sums = part if sums is None else sums + part
            other[:, start - low:start - low + WIDTH] = sums[:half]
            own[:, start - low:start - low + WIDTH] = sums[half:]

    shape = (half, high - low)
    depth = turned.shape[1]
    return call(
        kernel, [held(shape, f32), held(shape, f32)], [VMEM_SPACE] * (1 + len(flats)),
        flops=2 * RANK * depth * (high - low), moved=2 * depth * (high - low),
    )(turned, *flats)


def finish(own, came, y_local, z_local):
    half = own[0].shape[0]
    pieces = len(own)
    cells = y_local // pieces
    stride = y_local + 1
    step = min(half, 32)

    def kernel(*refs):
        out, scratch, sems = refs[-3:]
        rounded = scratch[1]
        spread = scratch[0]
        copies = []
        for start in range(0, half, step):
            for y_cell in range(y_local):
                k, at = y_cell // cells, y_cell % cells * z_local
                spread[pl.ds(start * stride + y_cell, step, stride=stride), :] = (
                    refs[k][start:start + step, at:at + z_local]
                    + refs[pieces + k][start:start + step, at:at + z_local]
                )
            for r in range(start, start + step):
                rounded[r] = spread[r * stride:r * stride + y_local, :].astype(bf16)
            copy = pltpu.make_async_copy(
                rounded.at[pl.ds(start, step)], out.at[pl.ds(start, step)], sems.at[start // step]
            )
            copy.start()
            copies.append(copy)
        for copy in copies:
            copy.wait()

    return call(
        lambda *refs: kernel(*refs[:-3], (refs[-3], refs[-2]), refs[-1]),
        jax.ShapeDtypeStruct((half, y_local, z_local), bf16), [VMEM_SPACE] * (2 * pieces),
        out_specs=ANY_SPACE, moved=10 * half * y_local * z_local,
        scratch_shapes=[
            pltpu.VMEM((half * stride, z_local), f32), pltpu.VMEM((half, y_local, z_local), bf16),
            pltpu.SemaphoreType.DMA((half // step,)),
        ],
    )(*own, *came)


def local(field, sketch_seeds):
    x_local, y_local, z_local = field.shape
    count = lax.axis_size("yz")
    inner = 2 if count % 2 == 0 else 1
    outer = count // inner
    chunk = x_local // count

    def neighbour(value):
        return lax.ppermute(value, "yz", [(i, i ^ 1) for i in range(count)])

    def shift(value, d):
        pairs = [(i, (i // inner + d) % outer * inner + i % inner) for i in range(count)]
        return lax.ppermute(value, "yz", pairs)

    def other_core(value):
        return lax.ppermute(value, "gx", [(0, 1), (1, 0)])

    sizes = (outer, inner, chunk)
    order = sorted(range(1, outer), key=lambda d: -min(d, outer - d)) + [0]
    cut = (outer + 1) // 2
    groups = [group for group in (order[:cut], order[cut:]) if group]
    wanted = [(d, 1) for d in order if inner == 2] + [(d, 0) for d in order]
    source, flats, sends, tables, at = field, [], [], None, 0
    if inner == 2:
        for group in groups:
            (rows,), flat, source, tables = sketch_chunks(
                source, sketch_seeds, wanted, at, len(group), sizes, True, tables
            )
            sends.append(neighbour(rows))
            at += len(group)
            flats.append(flat)
    parts = []
    for k, group in enumerate(groups):
        kept, flat, source, tables = sketch_chunks(
            source, sketch_seeds, wanted, at, len(group), sizes, False, tables
        )
        at += len(group)
        flats.append(flat)
        if inner == 2:
            kept = merge(kept, sends[k])
        for j, d in enumerate(group):
            parts.append(shift(kept[j], d) if d else kept[j])
    own = total_of(parts)
    chunks = [None] * count
    near = [0] + sorted(range(1, outer), key=lambda d: min(d, outer - d))
    for d in near:
        came = shift(own, d) if d else own
        chunks[d * inner] = came
        if inner == 2:
            chunks[d * inner + 1] = neighbour(came)
    gram = gram_of(chunks)
    came = other_core(gram)
    inverse = inverse_factor(gram, came)
    places = [wanted.index(((outer - k // inner) % outer, k % inner)) for k in range(count)]
    basis, turned = solve_rows(chunks, inverse, sizes, places)
    columns = y_local * z_local
    own_parts, came_parts = [], []
    for k in range(PIECES):
        other, mine = product(
            turned, flats, columns * k // PIECES, columns * (k + 1) // PIECES
        )
        came_parts.append(other_core(other))
        own_parts.append(mine)
    core = finish(own_parts, came_parts, y_local, z_local)
    return (basis, core)


PIECES = 4


def solution(mesh):
    in_specs = (P(("grp", "gx"), "yz", None), P("grp"))
    out_specs = (P(("grp", "gx"), None), P(("grp", "gx"), "yz", None))

    return jax.shard_map(local, mesh=mesh, in_specs=in_specs, out_specs=out_specs, check_vma=False)
```

```python
import jax
import jax.numpy as jnp
from jax import lax
from jax.experimental import pallas as pl
from jax.experimental.pallas import tpu as pltpu
from jax.sharding import PartitionSpec as P

RANK = 256
prime = 32749
f32, bf16, i32 = jnp.float32, jnp.bfloat16, jnp.int32


def remainder(value):
    quotient = (value.astype(f32) * (1.0 / prime)).astype(i32)
    rest = value - quotient * prime
    rest = jnp.where(rest < 0, rest + prime, rest)
    return jnp.where(rest >= prime, rest - prime, rest)


def omega_table(a, b, c, start, count):
    place = start + 1 + lax.broadcasted_iota(i32, (count, 1), 0)
    column = 1 + lax.broadcasted_iota(i32, (1, RANK), 1)
    first = remainder(a * place)
    second = remainder(b * column + c)
    square = remainder(place * place)
    third = remainder(c * column)
    mixed = remainder(remainder(first * second) + remainder(square * third))
    return mixed.astype(f32) * (2.0 / prime) - 1.0


LIMIT = 14 << 20
VMEM_SPACE = pl.BlockSpec(memory_space=pltpu.VMEM)
SMEM_SPACE = pl.BlockSpec(memory_space=pltpu.SMEM)
ANY_SPACE = pl.BlockSpec(memory_space=pl.ANY)
HBM_SPACE = pl.BlockSpec(memory_space=pltpu.HBM)
SUB = 64


def held(shape, dtype):
    return pltpu.VMEM(shape, dtype)


def call(kernel, out_shape, in_specs, flops=0, moved=0, **more):
    return pl.pallas_call(
        kernel,
        out_shape=out_shape,
        in_specs=in_specs,
        compiler_params=pltpu.CompilerParams(vmem_limit_bytes=LIMIT),
        cost_estimate=pl.CostEstimate(flops=flops, bytes_accessed=moved, transcendentals=0),
        **more,
    )


CELLS = 4


def sketch_chunks(field, seeds, wanted, follow, sizes, joined, carried=None):
    outer, inner, chunk = sizes
    _, y_local, z_local = field.shape
    sub = min(SUB, chunk)
    stride = y_local + 1
    parts = chunk // sub
    span = len(wanted)
    total = span * chunk
    opening = carried is None

    def kernel(*refs):
        refs = list(refs)
        field_ref, sems = refs.pop(0), refs.pop()
        if opening:
            seeds_ref, rows = refs.pop(0), refs.pop()
        else:
            rows, omega_z, omega_y = refs.pop(0), refs.pop(0), refs.pop(0)
        outs = [refs.pop(0) for _ in range(1 if joined else span)]
        flat = refs.pop(0)
        later = refs.pop(0) if follow else None
        if opening:
            omega_z, omega_y = refs.pop(0), refs.pop(0)
        me = lax.axis_index("yz")
        o, y = me // inner, me % inner
        moves = [(pair, rows, k) for k, pair in enumerate(wanted) if opening]
        moves += [(pair, later, k) for k, pair in enumerate(follow)]
        copies = []
        for (d, flip), target, k in moves:
            chosen = lax.rem(o + d, outer) * inner + (inner - 1 - y if flip else y)
            copy = pltpu.make_async_copy(
                field_ref.at[pl.ds(chosen * chunk, chunk)],
                target.at[pl.ds(k * chunk, chunk)],
                sems.at[len(copies)],
            )
            copy.start()
            copies.append(copy)
        if opening:
            omega_z[...] = omega_table(
                seeds_ref[3], seeds_ref[4], seeds_ref[5], 0, z_local
            ).astype(bf16)
            omega_y[...] = omega_table(
                seeds_ref[0], seeds_ref[1], seeds_ref[2], me * y_local, y_local
            )
        scratch = refs
        table_z = omega_z[...]

        def spread(block):
            if opening and block % parts == 0:
                copies[block // parts].wait()
            for x in range(sub):
                scratch[block % 2][x * stride:x * stride + y_local, :] = (
                    rows[block * sub + x].astype(f32)
                )

        spread(0)
        for block in range(span * parts):
            if block + 1 < span * parts:
                spread(block + 1)
            low = block * sub
            sums = None
            for y_cell in range(0, y_local, CELLS):
                cells = []
                for y_at in range(y_cell, y_cell + CELLS):
                    cell = scratch[block % 2][pl.ds(y_at, sub, stride=stride), :].astype(bf16)
                    flat[low:low + sub, y_at * z_local:(y_at + 1) * z_local] = cell
                    cells.append(cell)
                parted = jnp.dot(
                    jnp.concatenate(cells, axis=0), table_z, preferred_element_type=f32
                )
                for k in range(CELLS):
                    part = parted[k * sub:(k + 1) * sub] * omega_y[y_cell + k:y_cell + k + 1, :]
                    sums = part if sums is None else sums + part
            if joined:
                outs[0][low:low + sub, :] = sums
            else:
                start = block % parts * sub
                outs[block // parts][start:start + sub, :] = sums
        for copy in copies[span if opening else 0:]:
            copy.wait()

    count = 1 if joined else span
    shape = held((total if joined else chunk, RANK), f32)
    out_shape = [shape] * count + [held((total, y_local * z_local), bf16)]
    scratch_shapes = [pltpu.VMEM((sub * stride, z_local), f32)] * 2
    operands = [pltpu.with_memory_space_constraint(field, pltpu.HBM)]
    if follow:
        out_shape.append(held((len(follow) * chunk, y_local, z_local), bf16))
    if opening:
        operands.append(seeds)
        in_specs = [HBM_SPACE, SMEM_SPACE]
        out_shape += [held((z_local, RANK), bf16), held((y_local, RANK), f32)]
        scratch_shapes.append(pltpu.VMEM((total, y_local, z_local), bf16))
    else:
        operands += carried
        in_specs = [HBM_SPACE] + [VMEM_SPACE] * 3
    copies = len(follow) + (span if opening else 0)
    scratch_shapes.append(pltpu.SemaphoreType.DMA((max(copies, 1),)))
    result = call(
        kernel, out_shape, in_specs,
        flops=2 * total * y_local * z_local * RANK, moved=2 * total * y_local * z_local,
        scratch_shapes=scratch_shapes,
    )(*operands)
    coming = list(result[count + 1:count + 2]) if follow else []
    tables = list(result[-2:]) if opening else carried[1:]
    return result[:count], result[count], coming + tables


def split3(value):
    high = value.astype(bf16)
    rest = value - high.astype(f32)
    middle = rest.astype(bf16)
    return high, middle, (rest - middle.astype(f32)).astype(bf16)


PANEL = 32


def inverse_factor_kernel(gram, came, out, state):
    size = gram.shape[0]
    state[...] = gram[...] + came[...]
    lane = lax.broadcasted_iota(i32, (8, 128), 1)
    row = lax.broadcasted_iota(i32, (8, 128), 0)
    zero = jnp.where(lane < 0, 1.0, 0.0).astype(f32)
    groups = PANEL // 8

    def over_rows(value, i):
        return jnp.broadcast_to(value[i:i + 1], (8, 128))

    def over_lanes(value, i):
        return jnp.broadcast_to(value[:, i:i + 1], (8, 128))

    for low in range(0, size, PANEL):
        high = low + PANEL
        tile, offset = low // 128, low % 128
        rows = [
            [state[low + 8 * q:low + 8 * q + 8, 128 * k:128 * k + 128] for q in range(groups)]
            for k in range(2)
        ]
        rows.append(
            [jnp.where(lane == row + (offset + 8 * q), 1.0, 0.0).astype(f32) for q in range(groups)]
        )
        done = [[None] * groups for _ in range(3)]
        for g in range(groups):
            base = offset + 8 * g
            column = [
                {q: over_lanes(rows[tile][q], base + m) + zero for q in range(g, groups)}
                for m in range(8)
            ]
            scales, ratios = jnp.zeros((8, 128), f32), jnp.zeros((8, 128), f32)
            for i in range(0, 8, 2):
                d11, d12 = over_rows(column[i][g], i), over_rows(column[i + 1][g], i)
                d22 = over_rows(column[i + 1][g], i + 1)
                inverse = pl.reciprocal(d11 * d22 - d12 * d12)
                k11, k12, k22 = d22 * inverse, d12 * inverse, d11 * inverse
                ratio = d12 * pl.reciprocal(d11)
                root1, root2 = lax.rsqrt(d11), lax.rsqrt(d22 - ratio * d12)
                scales = jnp.where(row == i, root1, jnp.where(row == i + 1, root2, scales))
                ratios = jnp.where(row == i + 1, ratio, ratios)
                left, right = dict(column[i]), dict(column[i + 1])
                left[g] = jnp.where(row > i + 1, left[g], 0.0)
                right[g] = jnp.where(row > i + 1, right[g], 0.0)
                for m in range(i + 2, 8):
                    a, b = over_rows(column[m][g], i), over_rows(column[m][g], i + 1)
                    first, second = k11 * a - k12 * b, k22 * b - k12 * a
                    for q in range(g, groups):
                        column[m][q] = column[m][q] - (left[q] * first + right[q] * second)
                for k in range(3):
                    a, b = over_rows(rows[k][g], i), over_rows(rows[k][g], i + 1)
                    first, second = k11 * a - k12 * b, k22 * b - k12 * a
                    for q in range(g if i + 2 < 8 else g + 1, groups):
                        rows[k][q] = rows[k][q] - (left[q] * first + right[q] * second)
            for k in range(3):
                above = pltpu.roll(rows[k][g], 1, 0)
                done[k][g] = (rows[k][g] - ratios * above) * scales
        factor = [jnp.concatenate(part, axis=0) for part in done]
        lanes = lax.broadcasted_iota(i32, (PANEL, 128), 1)
        inside = (lanes >= offset) & (lanes < offset + PANEL)
        mixed = list(factor[:2])
        mixed[tile] = jnp.where(inside, factor[2], factor[tile])
        for k in range(2):
            if k < tile:
                value = mixed[k]
            elif k == tile:
                value = jnp.where(lanes < offset + PANEL, mixed[k], 0.0)
            else:
                value = jnp.zeros((PANEL, 128), f32)
            out[low:high, 128 * k:128 * (k + 1)] = value
        if high < size:
            start = high // 128 * 128
            h, m, l = split3(jnp.concatenate(factor[:2], axis=1)[:, start:])
            eh, em, el = split3(jnp.concatenate(mixed, axis=1))
            left = jnp.concatenate([h, h, m, m, h, l], axis=0)
            right = jnp.concatenate([eh, em, eh, em, el, eh], axis=0)
            update = lax.dot_general(
                left, right, (((0,), (0,)), ((), ())), preferred_element_type=f32
            )
            columns = lax.broadcasted_iota(i32, (size - high, size), 1)
            rest = jnp.where((columns >= low) & (columns < high), 0.0, state[high:, :])
            state[high:, :] = rest - update[high - start:, :]


def inverse_factor(gram, came):
    return call(
        inverse_factor_kernel, held(gram.shape, f32), [VMEM_SPACE] * 2,
        flops=3 * gram.shape[0] ** 3, moved=8 * gram.shape[0] ** 2,
        scratch_shapes=[pltpu.VMEM(gram.shape, f32)],
    )(gram, came)


def merge(kept, came):
    chunk = kept[0].shape[0]

    def kernel(*refs):
        came_ref = refs[len(kept)]
        for k in range(len(kept)):
            refs[len(kept) + 1 + k][...] = refs[k][...] + came_ref[k * chunk:(k + 1) * chunk, :]

    return call(
        kernel, [held(kept[0].shape, f32)] * len(kept), [VMEM_SPACE] * (len(kept) + 1),
        flops=came.size, moved=12 * came.size,
    )(*kept, came)


def total_of(parts):
    def kernel(*refs):
        sums = refs[0][...]
        for ref in refs[1:-1]:
            sums = sums + ref[...]
        refs[-1][...] = sums

    return call(
        kernel, held(parts[0].shape, f32), [VMEM_SPACE] * len(parts),
        flops=parts[0].size * len(parts), moved=4 * parts[0].size * len(parts),
    )(*parts)


def gram_of(chunks):
    chunk = chunks[0].shape[0]
    total = len(chunks) * chunk

    def kernel(*refs):
        rows_refs, (out, terms) = refs[:-2], refs[-2:]
        for k, ref in enumerate(rows_refs):
            for j, term in enumerate(split3(ref[...])):
                terms[k * chunk:(k + 1) * chunk, j * RANK:(j + 1) * RANK] = term
        over_rows = (((0,), (0,)), ((), ()))
        first = lax.dot_general(
            terms[:, :RANK], terms[...], over_rows, preferred_element_type=f32
        )
        middle = terms[:, RANK:2 * RANK]
        second = lax.dot_general(middle, middle, over_rows, preferred_element_type=f32)
        mixed = first[:, RANK:2 * RANK] + first[:, 2 * RANK:]
        out[...] = first[:, :RANK] + (second + (mixed + mixed.T))

    return call(
        kernel, held((RANK, RANK), f32), [VMEM_SPACE] * len(chunks),
        flops=8 * total * RANK ** 2, moved=4 * total * RANK,
        scratch_shapes=[pltpu.VMEM((total, 3 * RANK), bf16)],
    )(*chunks)


def split2(value):
    high = value.astype(bf16)
    return high, (value - high.astype(f32)).astype(bf16)


def solve_rows(chunks, inverse, sizes, places):
    outer, inner, chunk = sizes
    total = len(chunks) * chunk
    half = RANK // 2

    def kernel(inverse_ref, *refs):
        rows_refs, (basis, turned, rounded) = refs[:-3], refs[-3:]
        me = lax.axis_index("yz")
        o, y = me // inner, me % inner
        high, low = split2(inverse_ref[...])
        right = jnp.concatenate([high, high, low], axis=1)
        for k in range(outer * inner):
            d, flip = k // inner, k % inner
            high, low = split2(rows_refs[k][...])
            left = jnp.concatenate([high, low, high], axis=1)
            value = lax.dot_general(left, right, (((1,), (1,)), ((), ())), preferred_element_type=f32)
            chosen = lax.rem(o + outer - d, outer) * inner + (inner - 1 - y if flip else y)
            basis[pl.ds(pl.multiple_of(chosen * chunk, chunk), chunk), :] = value
            rounded[places[k] * chunk:(places[k] + 1) * chunk, :] = value
        step = 128
        for start in range(0, total, step):
            block = rounded[start:start + step, :].T.astype(bf16)
            first = lax.axis_index("gx") == 0
            turned[:half, start:start + step] = jnp.where(first, block[half:], block[:half])
            turned[half:, start:start + step] = jnp.where(first, block[:half], block[half:])

    return call(
        kernel, [held((total, RANK), f32), held((RANK, total), bf16)],
        [VMEM_SPACE] * (1 + len(chunks)),
        flops=6 * total * RANK ** 2, moved=8 * total * RANK,
        scratch_shapes=[pltpu.VMEM((total, RANK), f32)],
    )(inverse, *chunks)


WIDTH = 256


def product(turned, flats, low, high):
    half = RANK // 2

    def kernel(turned_ref, *refs):
        flat_refs, (other, own) = refs[:-2], refs[-2:]
        for start in range(low, high, WIDTH):
            sums, depth = None, 0
            for flat in flat_refs:
                part = jnp.dot(
                    turned_ref[:, depth:depth + flat.shape[0]], flat[:, start:start + WIDTH],
                    preferred_element_type=f32,
                )
                depth += flat.shape[0]
                sums = part if sums is None else sums + part
            other[:, start - low:start - low + WIDTH] = sums[:half]
            own[:, start - low:start - low + WIDTH] = sums[half:]

    shape = (half, high - low)
    depth = turned.shape[1]
    return call(
        kernel, [held(shape, f32), held(shape, f32)], [VMEM_SPACE] * (1 + len(flats)),
        flops=2 * RANK * depth * (high - low), moved=2 * depth * (high - low),
    )(turned, *flats)


def finish(own, came, y_local, z_local):
    half = own[0].shape[0]
    pieces = len(own)
    cells = y_local // pieces
    stride = y_local + 1
    step = min(half, 32)

    def kernel(*refs):
        out, scratch, sems = refs[-3:]
        rounded = scratch[1]
        spread = scratch[0]
        copies = []
        for start in range(0, half, step):
            for y_cell in range(y_local):
                k, at = y_cell // cells, y_cell % cells * z_local
                spread[pl.ds(start * stride + y_cell, step, stride=stride), :] = (
                    refs[k][start:start + step, at:at + z_local]
                    + refs[pieces + k][start:start + step, at:at + z_local]
                )
            for r in range(start, start + step):
                rounded[r] = spread[r * stride:r * stride + y_local, :].astype(bf16)
            copy = pltpu.make_async_copy(
                rounded.at[pl.ds(start, step)], out.at[pl.ds(start, step)], sems.at[start // step]
            )
            copy.start()
            copies.append(copy)
        for copy in copies:
            copy.wait()

    return call(
        lambda *refs: kernel(*refs[:-3], (refs[-3], refs[-2]), refs[-1]),
        jax.ShapeDtypeStruct((half, y_local, z_local), bf16), [VMEM_SPACE] * (2 * pieces),
        out_specs=ANY_SPACE, moved=10 * half * y_local * z_local,
        scratch_shapes=[
            pltpu.VMEM((half * stride, z_local), f32), pltpu.VMEM((half, y_local, z_local), bf16),
            pltpu.SemaphoreType.DMA((half // step,)),
        ],
    )(*own, *came)


def local(field, sketch_seeds):
    x_local, y_local, z_local = field.shape
    count = lax.axis_size("yz")
    inner = 2 if count % 2 == 0 else 1
    outer = count // inner
    chunk = x_local // count

    def neighbour(value):
        return lax.ppermute(value, "yz", [(i, i ^ 1) for i in range(count)])

    def shift(value, d):
        pairs = [(i, (i // inner + d) % outer * inner + i % inner) for i in range(count)]
        return lax.ppermute(value, "yz", pairs)

    def other_core(value):
        return lax.ppermute(value, "gx", [(0, 1), (1, 0)])

    sizes = (outer, inner, chunk)
    order = sorted(range(1, outer), key=lambda d: -min(d, outer - d)) + [0]
    cut = (outer + 1) // 2
    groups = [group for group in (order[:cut], order[cut:]) if group]
    turns = [(group, 1) for group in groups if inner == 2] + [(group, 0) for group in groups]
    turns = [[(d, flip) for d in group] for group, flip in turns]
    wanted = [pair for pairs in turns for pair in pairs]
    flats, sends, carried, turn = [], [], None, 0
    if inner == 2:
        for _ in range(len(groups)):
            (rows,), flat, carried = sketch_chunks(
                field, sketch_seeds, turns[turn], turns[turn + 1], sizes, True, carried
            )
            sends.append(neighbour(rows))
            turn += 1
            flats.append(flat)
    parts = []
    for k, group in enumerate(groups):
        follow = turns[turn + 1] if turn + 1 < len(turns) else []
        kept, flat, carried = sketch_chunks(
            field, sketch_seeds, turns[turn], follow, sizes, False, carried
        )
        turn += 1
        flats.append(flat)
        if inner == 2:
            kept = merge(kept, sends[k])
        for j, d in enumerate(group):
            parts.append(shift(kept[j], d) if d else kept[j])
    own = total_of(parts)
    chunks = [None] * count
    near = [0] + sorted(range(1, outer), key=lambda d: min(d, outer - d))
    for d in near:
        came = shift(own, d) if d else own
        chunks[d * inner] = came
        if inner == 2:
            chunks[d * inner + 1] = neighbour(came)
    gram = gram_of(chunks)
    came = other_core(gram)
    inverse = inverse_factor(gram, came)
    places = [wanted.index(((outer - k // inner) % outer, k % inner)) for k in range(count)]
    basis, turned = solve_rows(chunks, inverse, sizes, places)
    columns = y_local * z_local
    own_parts, came_parts = [], []
    for k in range(PIECES):
        other, mine = product(
            turned, flats, columns * k // PIECES, columns * (k + 1) // PIECES
        )
        came_parts.append(other_core(other))
        own_parts.append(mine)
    core = finish(own_parts, came_parts, y_local, z_local)
    return (basis, core)


PIECES = 4


def solution(mesh):
    in_specs = (P(("grp", "gx"), "yz", None), P("grp"))
    out_specs = (P(("grp", "gx"), None), P(("grp", "gx"), "yz", None))

    return jax.shard_map(local, mesh=mesh, in_specs=in_specs, out_specs=out_specs, check_vma=False)
```

```python
import jax
import jax.numpy as jnp
from jax import lax
from jax.experimental import pallas as pl
from jax.experimental.pallas import tpu as pltpu
from jax.sharding import PartitionSpec as P

RANK = 256
prime = 32749
f32, bf16, i32 = jnp.float32, jnp.bfloat16, jnp.int32


def remainder(value):
    quotient = (value.astype(f32) * (1.0 / prime)).astype(i32)
    rest = value - quotient * prime
    rest = jnp.where(rest < 0, rest + prime, rest)
    return jnp.where(rest >= prime, rest - prime, rest)


def omega_table(a, b, c, start, count):
    place = start + 1 + lax.broadcasted_iota(i32, (count, 1), 0)
    column = 1 + lax.broadcasted_iota(i32, (1, RANK), 1)
    first = remainder(a * place)
    second = remainder(b * column + c)
    square = remainder(place * place)
    third = remainder(c * column)
    mixed = remainder(remainder(first * second) + remainder(square * third))
    return mixed.astype(f32) * (2.0 / prime) - 1.0


LIMIT = 14 << 20
VMEM_SPACE = pl.BlockSpec(memory_space=pltpu.VMEM)
ANY_SPACE = pl.BlockSpec(memory_space=pl.ANY)
HBM_SPACE = pl.BlockSpec(memory_space=pltpu.HBM)
SUB = 64


def held(shape, dtype):
    return pltpu.VMEM(shape, dtype)


def call(kernel, out_shape, in_specs, flops=0, moved=0, **more):
    return pl.pallas_call(
        kernel,
        out_shape=out_shape,
        in_specs=in_specs,
        compiler_params=pltpu.CompilerParams(vmem_limit_bytes=LIMIT),
        cost_estimate=pl.CostEstimate(flops=flops, bytes_accessed=moved, transcendentals=0),
        **more,
    )


CELLS = 4


def sketch_chunks(field, seeds, wanted, follow, sizes, joined, carried=None):
    outer, inner, chunk = sizes
    _, y_local, z_local = field.shape
    sub = min(SUB, chunk)
    stride = y_local + 1
    parts = chunk // sub
    piece = min(32, sub)
    span = len(wanted)
    total = span * chunk
    opening = carried is None

    def kernel(*refs):
        refs = list(refs)
        field_ref, sems = refs.pop(0), refs.pop()
        if opening:
            seeds_hbm, seeds_ref, rows = refs.pop(0), refs.pop(), refs.pop()
        else:
            rows, omega_z, omega_y = refs.pop(0), refs.pop(0), refs.pop(0)
        outs = [refs.pop(0) for _ in range(1 if joined else span)]
        flat = refs.pop(0)
        later = refs.pop(0) if follow else None
        if opening:
            omega_z, omega_y = refs.pop(0), refs.pop(0)
        me = lax.axis_index("yz")
        o, y = me // inner, me % inner
        moves = [(pair, rows, k) for k, pair in enumerate(wanted) if opening]
        moves += [(pair, later, k) for k, pair in enumerate(follow)]
        copies = []
        for (d, flip), target, k in moves:
            chosen = lax.rem(o + d, outer) * inner + (inner - 1 - y if flip else y)
            for start in range(0, chunk, piece):
                copy = pltpu.make_async_copy(
                    field_ref.at[pl.ds(chosen * chunk + start, piece)],
                    target.at[pl.ds(k * chunk + start, piece)],
                    sems.at[len(copies)],
                )
                copy.start()
                copies.append(copy)
        if opening:
            seeds_copy = pltpu.make_async_copy(seeds_hbm, seeds_ref, sems.at[len(copies)])
            seeds_copy.start()
            seeds_copy.wait()
            omega_z[...] = omega_table(
                seeds_ref[3], seeds_ref[4], seeds_ref[5], 0, z_local
            ).astype(bf16)
            omega_y[...] = omega_table(
                seeds_ref[0], seeds_ref[1], seeds_ref[2], me * y_local, y_local
            )
        scratch = refs
        table_z = omega_z[...]

        def spread(block):
            if opening:
                for k in range(block * sub // piece, (block + 1) * sub // piece):
                    copies[k].wait()
            for x in range(sub):
                scratch[block % 2][x * stride:x * stride + y_local, :] = (
                    rows[block * sub + x].astype(f32)
                )

        spread(0)
        for block in range(span * parts):
            if block + 1 < span * parts:
                spread(block + 1)
            low = block * sub
            sums = None
            for y_cell in range(0, y_local, CELLS):
                cells = []
                for y_at in range(y_cell, y_cell + CELLS):
                    cell = scratch[block % 2][pl.ds(y_at, sub, stride=stride), :].astype(bf16)
                    flat[low:low + sub, y_at * z_local:(y_at + 1) * z_local] = cell
                    cells.append(cell)
                parted = jnp.dot(
                    jnp.concatenate(cells, axis=0), table_z, preferred_element_type=f32
                )
                for k in range(CELLS):
                    part = parted[k * sub:(k + 1) * sub] * omega_y[y_cell + k:y_cell + k + 1, :]
                    sums = part if sums is None else sums + part
            if joined:
                outs[0][low:low + sub, :] = sums
            else:
                start = block % parts * sub
                outs[block // parts][start:start + sub, :] = sums
        for copy in copies[total // piece if opening else 0:]:
            copy.wait()

    count = 1 if joined else span
    shape = held((total if joined else chunk, RANK), f32)
    out_shape = [shape] * count + [held((total, y_local * z_local), bf16)]
    scratch_shapes = [pltpu.VMEM((sub * stride, z_local), f32)] * 2
    operands = [pltpu.with_memory_space_constraint(field, pltpu.HBM)]
    if follow:
        out_shape.append(held((len(follow) * chunk, y_local, z_local), bf16))
    if opening:
        operands.append(pltpu.with_memory_space_constraint(seeds, pltpu.HBM))
        in_specs = [HBM_SPACE, HBM_SPACE]
        out_shape += [held((z_local, RANK), bf16), held((y_local, RANK), f32)]
        scratch_shapes.append(pltpu.VMEM((total, y_local, z_local), bf16))
        scratch_shapes.append(pltpu.SMEM(seeds.shape, i32))
    else:
        operands += carried
        in_specs = [HBM_SPACE] + [VMEM_SPACE] * 3
    copies = (len(follow) + (span if opening else 0)) * (chunk // piece)
    scratch_shapes.append(pltpu.SemaphoreType.DMA((copies + 1,)))
    result = call(
        kernel, out_shape, in_specs,
        flops=2 * total * y_local * z_local * RANK, moved=2 * total * y_local * z_local,
        scratch_shapes=scratch_shapes,
    )(*operands)
    coming = list(result[count + 1:count + 2]) if follow else []
    tables = list(result[-2:]) if opening else carried[1:]
    return result[:count], result[count], coming + tables


def split3(value):
    high = value.astype(bf16)
    rest = value - high.astype(f32)
    middle = rest.astype(bf16)
    return high, middle, (rest - middle.astype(f32)).astype(bf16)


PANEL = 32


def inverse_factor_kernel(gram, came, out, state):
    size = gram.shape[0]
    state[...] = gram[...] + came[...]
    lane = lax.broadcasted_iota(i32, (8, 128), 1)
    row = lax.broadcasted_iota(i32, (8, 128), 0)
    zero = jnp.where(lane < 0, 1.0, 0.0).astype(f32)
    groups = PANEL // 8

    def over_rows(value, i):
        return jnp.broadcast_to(value[i:i + 1], (8, 128))

    def over_lanes(value, i):
        return jnp.broadcast_to(value[:, i:i + 1], (8, 128))

    for low in range(0, size, PANEL):
        high = low + PANEL
        tile, offset = low // 128, low % 128
        rows = [
            [state[low + 8 * q:low + 8 * q + 8, 128 * k:128 * k + 128] for q in range(groups)]
            for k in range(2)
        ]
        rows.append(
            [jnp.where(lane == row + (offset + 8 * q), 1.0, 0.0).astype(f32) for q in range(groups)]
        )
        done = [[None] * groups for _ in range(3)]
        for g in range(groups):
            base = offset + 8 * g
            column = [
                {q: over_lanes(rows[tile][q], base + m) + zero for q in range(g, groups)}
                for m in range(8)
            ]
            scales, ratios = jnp.zeros((8, 128), f32), jnp.zeros((8, 128), f32)
            for i in range(0, 8, 2):
                d11, d12 = over_rows(column[i][g], i), over_rows(column[i + 1][g], i)
                d22 = over_rows(column[i + 1][g], i + 1)
                inverse = pl.reciprocal(d11 * d22 - d12 * d12)
                k11, k12, k22 = d22 * inverse, d12 * inverse, d11 * inverse
                ratio = d12 * pl.reciprocal(d11)
                root1, root2 = lax.rsqrt(d11), lax.rsqrt(d22 - ratio * d12)
                scales = jnp.where(row == i, root1, jnp.where(row == i + 1, root2, scales))
                ratios = jnp.where(row == i + 1, ratio, ratios)
                left, right = dict(column[i]), dict(column[i + 1])
                left[g] = jnp.where(row > i + 1, left[g], 0.0)
                right[g] = jnp.where(row > i + 1, right[g], 0.0)
                for m in range(i + 2, 8):
                    a, b = over_rows(column[m][g], i), over_rows(column[m][g], i + 1)
                    first, second = k11 * a - k12 * b, k22 * b - k12 * a
                    for q in range(g, groups):
                        column[m][q] = column[m][q] - (left[q] * first + right[q] * second)
                for k in range(3):
                    a, b = over_rows(rows[k][g], i), over_rows(rows[k][g], i + 1)
                    first, second = k11 * a - k12 * b, k22 * b - k12 * a
                    for q in range(g if i + 2 < 8 else g + 1, groups):
                        rows[k][q] = rows[k][q] - (left[q] * first + right[q] * second)
            for k in range(3):
                above = pltpu.roll(rows[k][g], 1, 0)
                done[k][g] = (rows[k][g] - ratios * above) * scales
        factor = [jnp.concatenate(part, axis=0) for part in done]
        lanes = lax.broadcasted_iota(i32, (PANEL, 128), 1)
        inside = (lanes >= offset) & (lanes < offset + PANEL)
        mixed = list(factor[:2])
        mixed[tile] = jnp.where(inside, factor[2], factor[tile])
        for k in range(2):
            if k < tile:
                value = mixed[k]
            elif k == tile:
                value = jnp.where(lanes < offset + PANEL, mixed[k], 0.0)
            else:
                value = jnp.zeros((PANEL, 128), f32)
            out[low:high, 128 * k:128 * (k + 1)] = value
        if high < size:
            start = high // 128 * 128
            h, m, l = split3(jnp.concatenate(factor[:2], axis=1)[:, start:])
            eh, em, el = split3(jnp.concatenate(mixed, axis=1))
            left = jnp.concatenate([h, h, m, m, h, l], axis=0)
            right = jnp.concatenate([eh, em, eh, em, el, eh], axis=0)
            update = lax.dot_general(
                left, right, (((0,), (0,)), ((), ())), preferred_element_type=f32
            )
            columns = lax.broadcasted_iota(i32, (size - high, size), 1)
            rest = jnp.where((columns >= low) & (columns < high), 0.0, state[high:, :])
            state[high:, :] = rest - update[high - start:, :]


def inverse_factor(gram, came):
    return call(
        inverse_factor_kernel, held(gram.shape, f32), [VMEM_SPACE] * 2,
        flops=3 * gram.shape[0] ** 3, moved=8 * gram.shape[0] ** 2,
        scratch_shapes=[pltpu.VMEM(gram.shape, f32)],
    )(gram, came)


def merge(kept, came):
    chunk = kept[0].shape[0]

    def kernel(*refs):
        came_ref = refs[len(kept)]
        for k in range(len(kept)):
            refs[len(kept) + 1 + k][...] = refs[k][...] + came_ref[k * chunk:(k + 1) * chunk, :]

    return call(
        kernel, [held(kept[0].shape, f32)] * len(kept), [VMEM_SPACE] * (len(kept) + 1),
        flops=came.size, moved=12 * came.size,
    )(*kept, came)


def total_of(parts):
    def kernel(*refs):
        sums = refs[0][...]
        for ref in refs[1:-1]:
            sums = sums + ref[...]
        refs[-1][...] = sums

    return call(
        kernel, held(parts[0].shape, f32), [VMEM_SPACE] * len(parts),
        flops=parts[0].size * len(parts), moved=4 * parts[0].size * len(parts),
    )(*parts)


def gram_of(chunks):
    chunk = chunks[0].shape[0]
    total = len(chunks) * chunk

    def kernel(*refs):
        rows_refs, (out, terms) = refs[:-2], refs[-2:]
        for k, ref in enumerate(rows_refs):
            for j, term in enumerate(split3(ref[...])):
                terms[k * chunk:(k + 1) * chunk, j * RANK:(j + 1) * RANK] = term
        over_rows = (((0,), (0,)), ((), ()))
        first = lax.dot_general(
            terms[:, :RANK], terms[...], over_rows, preferred_element_type=f32
        )
        middle = terms[:, RANK:2 * RANK]
        second = lax.dot_general(middle, middle, over_rows, preferred_element_type=f32)
        mixed = first[:, RANK:2 * RANK] + first[:, 2 * RANK:]
        out[...] = first[:, :RANK] + (second + (mixed + mixed.T))

    return call(
        kernel, held((RANK, RANK), f32), [VMEM_SPACE] * len(chunks),
        flops=8 * total * RANK ** 2, moved=4 * total * RANK,
        scratch_shapes=[pltpu.VMEM((total, 3 * RANK), bf16)],
    )(*chunks)


def split2(value):
    high = value.astype(bf16)
    return high, (value - high.astype(f32)).astype(bf16)


def solve_rows(chunks, inverse, sizes, places):
    outer, inner, chunk = sizes
    total = len(chunks) * chunk
    half = RANK // 2

    def kernel(inverse_ref, *refs):
        rows_refs, (basis, turned, rounded) = refs[:-3], refs[-3:]
        me = lax.axis_index("yz")
        o, y = me // inner, me % inner
        high, low = split2(inverse_ref[...])
        right = jnp.concatenate([high, high, low], axis=1)
        for k in range(outer * inner):
            d, flip = k // inner, k % inner
            high, low = split2(rows_refs[k][...])
            left = jnp.concatenate([high, low, high], axis=1)
            value = lax.dot_general(left, right, (((1,), (1,)), ((), ())), preferred_element_type=f32)
            chosen = lax.rem(o + outer - d, outer) * inner + (inner - 1 - y if flip else y)
            basis[pl.ds(pl.multiple_of(chosen * chunk, chunk), chunk), :] = value
            rounded[places[k] * chunk:(places[k] + 1) * chunk, :] = value
        step = 128
        for start in range(0, total, step):
            block = rounded[start:start + step, :].T.astype(bf16)
            first = lax.axis_index("gx") == 0
            turned[:half, start:start + step] = jnp.where(first, block[half:], block[:half])
            turned[half:, start:start + step] = jnp.where(first, block[:half], block[half:])

    return call(
        kernel, [held((total, RANK), f32), held((RANK, total), bf16)],
        [VMEM_SPACE] * (1 + len(chunks)),
        flops=6 * total * RANK ** 2, moved=8 * total * RANK,
        scratch_shapes=[pltpu.VMEM((total, RANK), f32)],
    )(inverse, *chunks)


WIDTH = 256


def product(turned, flats, low, high):
    half = RANK // 2

    def kernel(turned_ref, *refs):
        flat_refs, (other, own) = refs[:-2], refs[-2:]
        for start in range(low, high, WIDTH):
            sums, depth = None, 0
            for flat in flat_refs:
                part = jnp.dot(
                    turned_ref[:, depth:depth + flat.shape[0]], flat[:, start:start + WIDTH],
                    preferred_element_type=f32,
                )
                depth += flat.shape[0]
                sums = part if sums is None else sums + part
            other[:, start - low:start - low + WIDTH] = sums[:half]
            own[:, start - low:start - low + WIDTH] = sums[half:]

    shape = (half, high - low)
    depth = turned.shape[1]
    return call(
        kernel, [held(shape, f32), held(shape, f32)], [VMEM_SPACE] * (1 + len(flats)),
        flops=2 * RANK * depth * (high - low), moved=2 * depth * (high - low),
    )(turned, *flats)


def finish(own, came, y_local, z_local):
    half = own[0].shape[0]
    pieces = len(own)
    cells = y_local // pieces
    stride = y_local + 1
    step = min(half, 32)

    def kernel(*refs):
        out, scratch, sems = refs[-3:]
        rounded = scratch[1]
        spread = scratch[0]
        copies = []
        for start in range(0, half, step):
            for y_cell in range(y_local):
                k, at = y_cell // cells, y_cell % cells * z_local
                spread[pl.ds(start * stride + y_cell, step, stride=stride), :] = (
                    refs[k][start:start + step, at:at + z_local]
                    + refs[pieces + k][start:start + step, at:at + z_local]
                )
            for r in range(start, start + step):
                rounded[r] = spread[r * stride:r * stride + y_local, :].astype(bf16)
            copy = pltpu.make_async_copy(
                rounded.at[pl.ds(start, step)], out.at[pl.ds(start, step)], sems.at[start // step]
            )
            copy.start()
            copies.append(copy)
        for copy in copies:
            copy.wait()

    return call(
        lambda *refs: kernel(*refs[:-3], (refs[-3], refs[-2]), refs[-1]),
        jax.ShapeDtypeStruct((half, y_local, z_local), bf16), [VMEM_SPACE] * (2 * pieces),
        out_specs=ANY_SPACE, moved=10 * half * y_local * z_local,
        scratch_shapes=[
            pltpu.VMEM((half * stride, z_local), f32), pltpu.VMEM((half, y_local, z_local), bf16),
            pltpu.SemaphoreType.DMA((half // step,)),
        ],
    )(*own, *came)


def local(field, sketch_seeds):
    x_local, y_local, z_local = field.shape
    count = lax.axis_size("yz")
    inner = 2 if count % 2 == 0 else 1
    outer = count // inner
    chunk = x_local // count

    def neighbour(value):
        return lax.ppermute(value, "yz", [(i, i ^ 1) for i in range(count)])

    def shift(value, d):
        pairs = [(i, (i // inner + d) % outer * inner + i % inner) for i in range(count)]
        return lax.ppermute(value, "yz", pairs)

    def other_core(value):
        return lax.ppermute(value, "gx", [(0, 1), (1, 0)])

    sizes = (outer, inner, chunk)
    order = sorted(range(1, outer), key=lambda d: -min(d, outer - d)) + [0]
    groups = [group for group in (order[:1], order[1:-1], order[-1:] if outer > 1 else []) if group]
    turns = turns_of(len(groups), inner)
    pairs = [[(d, flip) for d in groups[k]] for k, flip in turns]
    wanted = [pair for some in pairs for pair in some]
    flats, sends, parts, carried = [], {}, [], None
    for turn, (k, flip) in enumerate(turns):
        follow = pairs[turn + 1] if turn + 1 < len(turns) else []
        made, flat, carried = sketch_chunks(
            field, sketch_seeds, pairs[turn], follow, sizes, flip == 1, carried
        )
        flats.append(flat)
        if flip:
            sends[k] = neighbour(made[0])
            continue
        kept = merge(made, sends[k]) if inner == 2 else made
        for j, d in enumerate(groups[k]):
            parts.append(shift(kept[j], d) if d else kept[j])
    own = total_of(parts)
    chunks = [None] * count
    near = [0] + sorted(range(1, outer), key=lambda d: min(d, outer - d))
    for d in near:
        came = shift(own, d) if d else own
        chunks[d * inner] = came
        if inner == 2:
            chunks[d * inner + 1] = neighbour(came)
    gram = gram_of(chunks)
    came = other_core(gram)
    inverse = inverse_factor(gram, came)
    places = [wanted.index(((outer - k // inner) % outer, k % inner)) for k in range(count)]
    basis, turned = solve_rows(chunks, inverse, sizes, places)
    columns = y_local * z_local
    own_parts, came_parts = [], []
    for k in range(PIECES):
        other, mine = product(
            turned, flats, columns * k // PIECES, columns * (k + 1) // PIECES
        )
        came_parts.append(other_core(other))
        own_parts.append(mine)
    core = finish(own_parts, came_parts, y_local, z_local)
    return (basis, core)


PIECES = 4


def turns_of(groups, inner):
    if inner == 1:
        return [(k, 0) for k in range(groups)]
    if groups < 3:
        return [(k, 1) for k in range(groups)] + [(k, 0) for k in range(groups)]
    return [(0, 1), (1, 1), (0, 0), (2, 1), (1, 0), (2, 0)]


def solution(mesh):
    in_specs = (P(("grp", "gx"), "yz", None), P("grp"))
    out_specs = (P(("grp", "gx"), None), P(("grp", "gx"), "yz", None))

    return jax.shard_map(local, mesh=mesh, in_specs=in_specs, out_specs=out_specs, check_vma=False)
```

```python
import jax
import jax.numpy as jnp
from jax import lax
from jax.experimental import pallas as pl
from jax.experimental.pallas import tpu as pltpu
from jax.sharding import PartitionSpec as P

RANK = 256
prime = 32749
f32, bf16, i32 = jnp.float32, jnp.bfloat16, jnp.int32


def remainder(value):
    quotient = (value.astype(f32) * (1.0 / prime)).astype(i32)
    rest = value - quotient * prime
    rest = jnp.where(rest < 0, rest + prime, rest)
    return jnp.where(rest >= prime, rest - prime, rest)


def omega_table(a, b, c, start, count):
    place = start + 1 + lax.broadcasted_iota(i32, (count, 1), 0)
    column = 1 + lax.broadcasted_iota(i32, (1, RANK), 1)
    first = remainder(a * place)
    second = remainder(b * column + c)
    square = remainder(place * place)
    third = remainder(c * column)
    mixed = remainder(remainder(first * second) + remainder(square * third))
    return mixed.astype(f32) * (2.0 / prime) - 1.0


LIMIT = 14 << 20
VMEM_SPACE = pl.BlockSpec(memory_space=pltpu.VMEM)
ANY_SPACE = pl.BlockSpec(memory_space=pl.ANY)
HBM_SPACE = pl.BlockSpec(memory_space=pltpu.HBM)
SUB = 64


def held(shape, dtype):
    return pltpu.VMEM(shape, dtype)


def call(kernel, out_shape, in_specs, flops=0, moved=0, **more):
    return pl.pallas_call(
        kernel,
        out_shape=out_shape,
        in_specs=in_specs,
        compiler_params=pltpu.CompilerParams(vmem_limit_bytes=LIMIT),
        cost_estimate=pl.CostEstimate(flops=flops, bytes_accessed=moved, transcendentals=0),
        **more,
    )


CELLS = 4


def sketch_chunks(field, seeds, wanted, follow, sizes, joined, carried=None):
    outer, inner, chunk = sizes
    _, y_local, z_local = field.shape
    sub = min(SUB, chunk)
    stride = y_local + 1
    parts = chunk // sub
    piece = min(32, sub)
    span = len(wanted)
    total = span * chunk
    opening = carried is None

    def kernel(*refs):
        refs = list(refs)
        field_ref, sems = refs.pop(0), refs.pop()
        if opening:
            seeds_hbm, seeds_ref, rows = refs.pop(0), refs.pop(), refs.pop()
        else:
            rows, omega_z, omega_y = refs.pop(0), refs.pop(0), refs.pop(0)
        outs = [refs.pop(0) for _ in range(1 if joined else span)]
        flat = refs.pop(0)
        later = refs.pop(0) if follow else None
        if opening:
            omega_z, omega_y = refs.pop(0), refs.pop(0)
        me = lax.axis_index("yz")
        o, y = me // inner, me % inner
        moves = [(pair, rows, k) for k, pair in enumerate(wanted) if opening]
        moves += [(pair, later, k) for k, pair in enumerate(follow)]
        copies = []
        for (d, flip), target, k in moves:
            chosen = lax.rem(o + d, outer) * inner + (inner - 1 - y if flip else y)
            for start in range(0, chunk, piece):
                copy = pltpu.make_async_copy(
                    field_ref.at[pl.ds(chosen * chunk + start, piece)],
                    target.at[pl.ds(k * chunk + start, piece)],
                    sems.at[len(copies)],
                )
                copy.start()
                copies.append(copy)

        def make_tables():
            omega_z[...] = omega_table(
                seeds_ref[3], seeds_ref[4], seeds_ref[5], 0, z_local
            ).astype(bf16)
            omega_y[...] = omega_table(
                seeds_ref[0], seeds_ref[1], seeds_ref[2], me * y_local, y_local
            )

        def make_rows():
            scratch = refs
            table_z = omega_z[...]

            def spread(block):
                if opening:
                    for k in range(block * sub // piece, (block + 1) * sub // piece):
                        copies[k].wait()
                for x in range(sub):
                    scratch[block % 2][x * stride:x * stride + y_local, :] = (
                        rows[block * sub + x].astype(f32)
                    )

            spread(0)
            for block in range(span * parts):
                if block + 1 < span * parts:
                    spread(block + 1)
                low = block * sub
                sums = None
                for y_cell in range(0, y_local, CELLS):
                    cells = []
                    for y_at in range(y_cell, y_cell + CELLS):
                        cell = scratch[block % 2][pl.ds(y_at, sub, stride=stride), :].astype(bf16)
                        flat[low:low + sub, y_at * z_local:(y_at + 1) * z_local] = cell
                        cells.append(cell)
                    parted = jnp.dot(
                        jnp.concatenate(cells, axis=0), table_z, preferred_element_type=f32
                    )
                    for k in range(CELLS):
                        part = parted[k * sub:(k + 1) * sub] * omega_y[y_cell + k:y_cell + k + 1, :]
                        sums = part if sums is None else sums + part
                if joined:
                    outs[0][low:low + sub, :] = sums
                else:
                    start = block % parts * sub
                    outs[block // parts][start:start + sub, :] = sums

        if opening:
            seeds_copy = pltpu.make_async_copy(seeds_hbm, seeds_ref, sems.at[len(copies)])
            seeds_copy.start()

        @pl.when(me >= 0)
        def compute():
            if opening:
                seeds_copy.wait()
                make_tables()
            make_rows()

        for copy in copies[total // piece if opening else 0:]:
            copy.wait()

    count = 1 if joined else span
    shape = held((total if joined else chunk, RANK), f32)
    out_shape = [shape] * count + [held((total, y_local * z_local), bf16)]
    scratch_shapes = [pltpu.VMEM((sub * stride, z_local), f32)] * 2
    operands = [pltpu.with_memory_space_constraint(field, pltpu.HBM)]
    if follow:
        out_shape.append(held((len(follow) * chunk, y_local, z_local), bf16))
    if opening:
        operands.append(pltpu.with_memory_space_constraint(seeds, pltpu.HBM))
        in_specs = [HBM_SPACE, HBM_SPACE]
        out_shape += [held((z_local, RANK), bf16), held((y_local, RANK), f32)]
        scratch_shapes.append(pltpu.VMEM((total, y_local, z_local), bf16))
        scratch_shapes.append(pltpu.SMEM(seeds.shape, i32))
    else:
        operands += carried
        in_specs = [HBM_SPACE] + [VMEM_SPACE] * 3
    copies = (len(follow) + (span if opening else 0)) * (chunk // piece)
    scratch_shapes.append(pltpu.SemaphoreType.DMA((copies + 1,)))
    result = call(
        kernel, out_shape, in_specs,
        flops=2 * total * y_local * z_local * RANK, moved=2 * total * y_local * z_local,
        scratch_shapes=scratch_shapes,
    )(*operands)
    coming = list(result[count + 1:count + 2]) if follow else []
    tables = list(result[-2:]) if opening else carried[1:]
    return result[:count], result[count], coming + tables


def split3(value):
    high = value.astype(bf16)
    rest = value - high.astype(f32)
    middle = rest.astype(bf16)
    return high, middle, (rest - middle.astype(f32)).astype(bf16)


PANEL = 32


def inverse_factor_kernel(gram, came, out, state):
    size = gram.shape[0]
    state[...] = gram[...] + came[...]
    lane = lax.broadcasted_iota(i32, (8, 128), 1)
    row = lax.broadcasted_iota(i32, (8, 128), 0)
    zero = jnp.where(lane < 0, 1.0, 0.0).astype(f32)
    groups = PANEL // 8

    def over_rows(value, i):
        return jnp.broadcast_to(value[i:i + 1], (8, 128))

    def over_lanes(value, i):
        return jnp.broadcast_to(value[:, i:i + 1], (8, 128))

    for low in range(0, size, PANEL):
        high = low + PANEL
        tile, offset = low // 128, low % 128
        rows = [
            [state[low + 8 * q:low + 8 * q + 8, 128 * k:128 * k + 128] for q in range(groups)]
            for k in range(2)
        ]
        rows.append(
            [jnp.where(lane == row + (offset + 8 * q), 1.0, 0.0).astype(f32) for q in range(groups)]
        )
        done = [[None] * groups for _ in range(3)]
        for g in range(groups):
            base = offset + 8 * g
            column = [
                {q: over_lanes(rows[tile][q], base + m) + zero for q in range(g, groups)}
                for m in range(8)
            ]
            scales, ratios = jnp.zeros((8, 128), f32), jnp.zeros((8, 128), f32)
            for i in range(0, 8, 2):
                d11, d12 = over_rows(column[i][g], i), over_rows(column[i + 1][g], i)
                d22 = over_rows(column[i + 1][g], i + 1)
                inverse = pl.reciprocal(d11 * d22 - d12 * d12)
                k11, k12, k22 = d22 * inverse, d12 * inverse, d11 * inverse
                ratio = d12 * pl.reciprocal(d11)
                root1, root2 = lax.rsqrt(d11), lax.rsqrt(d22 - ratio * d12)
                scales = jnp.where(row == i, root1, jnp.where(row == i + 1, root2, scales))
                ratios = jnp.where(row == i + 1, ratio, ratios)
                left, right = dict(column[i]), dict(column[i + 1])
                left[g] = jnp.where(row > i + 1, left[g], 0.0)
                right[g] = jnp.where(row > i + 1, right[g], 0.0)
                for m in range(i + 2, 8):
                    a, b = over_rows(column[m][g], i), over_rows(column[m][g], i + 1)
                    first, second = k11 * a - k12 * b, k22 * b - k12 * a
                    for q in range(g, groups):
                        column[m][q] = column[m][q] - (left[q] * first + right[q] * second)
                for k in range(3):
                    a, b = over_rows(rows[k][g], i), over_rows(rows[k][g], i + 1)
                    first, second = k11 * a - k12 * b, k22 * b - k12 * a
                    for q in range(g if i + 2 < 8 else g + 1, groups):
                        rows[k][q] = rows[k][q] - (left[q] * first + right[q] * second)
            for k in range(3):
                above = pltpu.roll(rows[k][g], 1, 0)
                done[k][g] = (rows[k][g] - ratios * above) * scales
        factor = [jnp.concatenate(part, axis=0) for part in done]
        lanes = lax.broadcasted_iota(i32, (PANEL, 128), 1)
        inside = (lanes >= offset) & (lanes < offset + PANEL)
        mixed = list(factor[:2])
        mixed[tile] = jnp.where(inside, factor[2], factor[tile])
        for k in range(2):
            if k < tile:
                value = mixed[k]
            elif k == tile:
                value = jnp.where(lanes < offset + PANEL, mixed[k], 0.0)
            else:
                value = jnp.zeros((PANEL, 128), f32)
            out[low:high, 128 * k:128 * (k + 1)] = value
        if high < size:
            start = high // 128 * 128
            h, m, l = split3(jnp.concatenate(factor[:2], axis=1)[:, start:])
            eh, em, el = split3(jnp.concatenate(mixed, axis=1))
            left = jnp.concatenate([h, h, m, m, h, l], axis=0)
            right = jnp.concatenate([eh, em, eh, em, el, eh], axis=0)
            update = lax.dot_general(
                left, right, (((0,), (0,)), ((), ())), preferred_element_type=f32
            )
            columns = lax.broadcasted_iota(i32, (size - high, size), 1)
            rest = jnp.where((columns >= low) & (columns < high), 0.0, state[high:, :])
            state[high:, :] = rest - update[high - start:, :]


def inverse_factor(gram, came):
    return call(
        inverse_factor_kernel, held(gram.shape, f32), [VMEM_SPACE] * 2,
        flops=3 * gram.shape[0] ** 3, moved=8 * gram.shape[0] ** 2,
        scratch_shapes=[pltpu.VMEM(gram.shape, f32)],
    )(gram, came)


def merge(kept, came):
    chunk = kept[0].shape[0]

    def kernel(*refs):
        came_ref = refs[len(kept)]
        for k in range(len(kept)):
            refs[len(kept) + 1 + k][...] = refs[k][...] + came_ref[k * chunk:(k + 1) * chunk, :]

    return call(
        kernel, [held(kept[0].shape, f32)] * len(kept), [VMEM_SPACE] * (len(kept) + 1),
        flops=came.size, moved=12 * came.size,
    )(*kept, came)


def total_of(parts):
    def kernel(*refs):
        sums = refs[0][...]
        for ref in refs[1:-1]:
            sums = sums + ref[...]
        refs[-1][...] = sums

    return call(
        kernel, held(parts[0].shape, f32), [VMEM_SPACE] * len(parts),
        flops=parts[0].size * len(parts), moved=4 * parts[0].size * len(parts),
    )(*parts)


def gram_of(chunks):
    chunk = chunks[0].shape[0]
    total = len(chunks) * chunk

    def kernel(*refs):
        rows_refs, (out, terms) = refs[:-2], refs[-2:]
        for k, ref in enumerate(rows_refs):
            for j, term in enumerate(split3(ref[...])):
                terms[k * chunk:(k + 1) * chunk, j * RANK:(j + 1) * RANK] = term
        over_rows = (((0,), (0,)), ((), ()))
        first = lax.dot_general(
            terms[:, :RANK], terms[...], over_rows, preferred_element_type=f32
        )
        middle = terms[:, RANK:2 * RANK]
        second = lax.dot_general(middle, middle, over_rows, preferred_element_type=f32)
        mixed = first[:, RANK:2 * RANK] + first[:, 2 * RANK:]
        out[...] = first[:, :RANK] + (second + (mixed + mixed.T))

    return call(
        kernel, held((RANK, RANK), f32), [VMEM_SPACE] * len(chunks),
        flops=8 * total * RANK ** 2, moved=4 * total * RANK,
        scratch_shapes=[pltpu.VMEM((total, 3 * RANK), bf16)],
    )(*chunks)


def split2(value):
    high = value.astype(bf16)
    return high, (value - high.astype(f32)).astype(bf16)


def solve_rows(chunks, inverse, sizes, places):
    outer, inner, chunk = sizes
    total = len(chunks) * chunk
    half = RANK // 2

    def kernel(inverse_ref, *refs):
        rows_refs, (basis, turned, rounded) = refs[:-3], refs[-3:]
        me = lax.axis_index("yz")
        o, y = me // inner, me % inner
        high, low = split2(inverse_ref[...])
        right = jnp.concatenate([high, high, low], axis=1)
        for k in range(outer * inner):
            d, flip = k // inner, k % inner
            high, low = split2(rows_refs[k][...])
            left = jnp.concatenate([high, low, high], axis=1)
            value = lax.dot_general(left, right, (((1,), (1,)), ((), ())), preferred_element_type=f32)
            chosen = lax.rem(o + outer - d, outer) * inner + (inner - 1 - y if flip else y)
            basis[pl.ds(pl.multiple_of(chosen * chunk, chunk), chunk), :] = value
            rounded[places[k] * chunk:(places[k] + 1) * chunk, :] = value
        step = 128
        for start in range(0, total, step):
            block = rounded[start:start + step, :].T.astype(bf16)
            first = lax.axis_index("gx") == 0
            turned[:half, start:start + step] = jnp.where(first, block[half:], block[:half])
            turned[half:, start:start + step] = jnp.where(first, block[:half], block[half:])

    return call(
        kernel, [held((total, RANK), f32), held((RANK, total), bf16)],
        [VMEM_SPACE] * (1 + len(chunks)),
        flops=6 * total * RANK ** 2, moved=8 * total * RANK,
        scratch_shapes=[pltpu.VMEM((total, RANK), f32)],
    )(inverse, *chunks)


WIDTH = 256


def product(turned, flats, low, high):
    half = RANK // 2

    def kernel(turned_ref, *refs):
        flat_refs, (other, own) = refs[:-2], refs[-2:]
        for start in range(low, high, WIDTH):
            cells = jnp.concatenate([flat[:, start:start + WIDTH] for flat in flat_refs], axis=0)
            sums = jnp.dot(turned_ref[...], cells, preferred_element_type=f32)
            other[:, start - low:start - low + WIDTH] = sums[:half]
            own[:, start - low:start - low + WIDTH] = sums[half:]

    shape = (half, high - low)
    depth = turned.shape[1]
    return call(
        kernel, [held(shape, f32), held(shape, f32)], [VMEM_SPACE] * (1 + len(flats)),
        flops=2 * RANK * depth * (high - low), moved=2 * depth * (high - low),
    )(turned, *flats)


def finish(own, came, y_local, z_local):
    half = own[0].shape[0]
    pieces = len(own)
    cells = y_local // pieces
    stride = y_local + 1
    step = min(half, 32)

    def kernel(*refs):
        out, scratch, sems = refs[-3:]
        rounded = scratch[1]
        spread = scratch[0]
        copies = []
        for start in range(0, half, step):
            for y_cell in range(y_local):
                k, at = y_cell // cells, y_cell % cells * z_local
                spread[pl.ds(start * stride + y_cell, step, stride=stride), :] = (
                    refs[k][start:start + step, at:at + z_local]
                    + refs[pieces + k][start:start + step, at:at + z_local]
                )
            for r in range(start, start + step):
                rounded[r] = spread[r * stride:r * stride + y_local, :].astype(bf16)
            copy = pltpu.make_async_copy(
                rounded.at[pl.ds(start, step)], out.at[pl.ds(start, step)], sems.at[start // step]
            )
            copy.start()
            copies.append(copy)
        for copy in copies:
            copy.wait()

    return call(
        lambda *refs: kernel(*refs[:-3], (refs[-3], refs[-2]), refs[-1]),
        jax.ShapeDtypeStruct((half, y_local, z_local), bf16), [VMEM_SPACE] * (2 * pieces),
        out_specs=ANY_SPACE, moved=10 * half * y_local * z_local,
        scratch_shapes=[
            pltpu.VMEM((half * stride, z_local), f32), pltpu.VMEM((half, y_local, z_local), bf16),
            pltpu.SemaphoreType.DMA((half // step,)),
        ],
    )(*own, *came)


def local(field, sketch_seeds):
    x_local, y_local, z_local = field.shape
    count = lax.axis_size("yz")
    inner = 2 if count % 2 == 0 else 1
    outer = count // inner
    chunk = x_local // count

    def neighbour(value):
        return lax.ppermute(value, "yz", [(i, i ^ 1) for i in range(count)])

    def shift(value, d):
        pairs = [(i, (i // inner + d) % outer * inner + i % inner) for i in range(count)]
        return lax.ppermute(value, "yz", pairs)

    def other_core(value):
        return lax.ppermute(value, "gx", [(0, 1), (1, 0)])

    sizes = (outer, inner, chunk)
    order = sorted(range(1, outer), key=lambda d: -min(d, outer - d)) + [0]
    groups = [group for group in (order[:1], order[1:-1], order[-1:] if outer > 1 else []) if group]
    turns = turns_of(len(groups), inner)
    pairs = [[(d, flip) for d in groups[k]] for k, flip in turns]
    wanted = [pair for some in pairs for pair in some]
    flats, sends, parts, carried = [], {}, [], None
    for turn, (k, flip) in enumerate(turns):
        follow = pairs[turn + 1] if turn + 1 < len(turns) else []
        made, flat, carried = sketch_chunks(
            field, sketch_seeds, pairs[turn], follow, sizes, flip == 1, carried
        )
        flats.append(flat)
        if flip:
            sends[k] = neighbour(made[0])
            continue
        kept = merge(made, sends[k]) if inner == 2 else made
        for j, d in enumerate(groups[k]):
            parts.append(shift(kept[j], d) if d else kept[j])
    own = total_of(parts)
    chunks = [None] * count
    near = [0] + sorted(range(1, outer), key=lambda d: min(d, outer - d))
    for d in near:
        came = shift(own, d) if d else own
        chunks[d * inner] = came
        if inner == 2:
            chunks[d * inner + 1] = neighbour(came)
    gram = gram_of(chunks)
    came = other_core(gram)
    inverse = inverse_factor(gram, came)
    places = [wanted.index(((outer - k // inner) % outer, k % inner)) for k in range(count)]
    basis, turned = solve_rows(chunks, inverse, sizes, places)
    columns = y_local * z_local
    own_parts, came_parts = [], []
    for k in range(PIECES):
        other, mine = product(
            turned, flats, columns * k // PIECES, columns * (k + 1) // PIECES
        )
        came_parts.append(other_core(other))
        own_parts.append(mine)
    core = finish(own_parts, came_parts, y_local, z_local)
    return (basis, core)


PIECES = 4


def turns_of(groups, inner):
    if inner == 1:
        return [(k, 0) for k in range(groups)]
    if groups < 3:
        return [(k, 1) for k in range(groups)] + [(k, 0) for k in range(groups)]
    return [(0, 1), (1, 1), (0, 0), (2, 1), (1, 0), (2, 0)]


def solution(mesh):
    in_specs = (P(("grp", "gx"), "yz", None), P("grp"))
    out_specs = (P(("grp", "gx"), None), P(("grp", "gx"), "yz", None))

    return jax.shard_map(local, mesh=mesh, in_specs=in_specs, out_specs=out_specs, check_vma=False)
```

```python
import jax
import jax.numpy as jnp
from jax import lax
from jax.experimental import pallas as pl
from jax.experimental.pallas import tpu as pltpu
from jax.sharding import PartitionSpec as P

RANK = 256
prime = 32749
f32, bf16, i32 = jnp.float32, jnp.bfloat16, jnp.int32


def remainder(value):
    quotient = (value.astype(f32) * (1.0 / prime)).astype(i32)
    rest = value - quotient * prime
    rest = jnp.where(rest < 0, rest + prime, rest)
    return jnp.where(rest >= prime, rest - prime, rest)


def omega_table(a, b, c, start, count):
    place = start + 1 + lax.broadcasted_iota(i32, (count, 1), 0)
    column = 1 + lax.broadcasted_iota(i32, (1, RANK), 1)
    first = remainder(a * place)
    second = remainder(b * column + c)
    square = remainder(place * place)
    third = remainder(c * column)
    mixed = remainder(remainder(first * second) + remainder(square * third))
    return mixed.astype(f32) * (2.0 / prime) - 1.0


LIMIT = 14 << 20
VMEM_SPACE = pl.BlockSpec(memory_space=pltpu.VMEM)
ANY_SPACE = pl.BlockSpec(memory_space=pl.ANY)
HBM_SPACE = pl.BlockSpec(memory_space=pltpu.HBM)
SUB = 64


def held(shape, dtype):
    return pltpu.VMEM(shape, dtype)


def call(kernel, out_shape, in_specs, flops=0, moved=0, **more):
    return pl.pallas_call(
        kernel,
        out_shape=out_shape,
        in_specs=in_specs,
        compiler_params=pltpu.CompilerParams(vmem_limit_bytes=LIMIT),
        cost_estimate=pl.CostEstimate(flops=flops, bytes_accessed=moved, transcendentals=0),
        **more,
    )


CELLS = 4


def sketch_chunks(field, seeds, wanted, follow, sizes, joined, carried=None):
    outer, inner, chunk = sizes
    _, y_local, z_local = field.shape
    sub = min(SUB, chunk)
    stride = y_local + 1
    parts = chunk // sub
    piece = min(32, sub)
    span = len(wanted)
    total = span * chunk
    opening = carried is None

    def kernel(*refs):
        refs = list(refs)
        field_ref, sems = refs.pop(0), refs.pop()
        if opening:
            seeds_hbm, seeds_ref, rows = refs.pop(0), refs.pop(), refs.pop()
        else:
            rows, omega_z, omega_y = refs.pop(0), refs.pop(0), refs.pop(0)
        outs = [refs.pop(0) for _ in range(1 if joined else span)]
        flat = refs.pop(0)
        later = refs.pop(0) if follow else None
        if opening:
            omega_z, omega_y = refs.pop(0), refs.pop(0)
        me = lax.axis_index("yz")
        o, y = me // inner, me % inner
        moves = [(pair, rows, k) for k, pair in enumerate(wanted) if opening]
        moves += [(pair, later, k) for k, pair in enumerate(follow)]
        copies = []
        for (d, flip), target, k in moves:
            chosen = lax.rem(o + d, outer) * inner + (inner - 1 - y if flip else y)
            for start in range(0, chunk, piece):
                copy = pltpu.make_async_copy(
                    field_ref.at[pl.ds(chosen * chunk + start, piece)],
                    target.at[pl.ds(k * chunk + start, piece)],
                    sems.at[len(copies)],
                )
                copy.start()
                copies.append(copy)

        def make_tables():
            omega_z[...] = omega_table(
                seeds_ref[3], seeds_ref[4], seeds_ref[5], 0, z_local
            ).astype(bf16)
            omega_y[...] = omega_table(
                seeds_ref[0], seeds_ref[1], seeds_ref[2], me * y_local, y_local
            )

        def make_rows():
            scratch = refs
            table_z = omega_z[...]

            def spread(block):
                if opening:
                    for k in range(block * sub // piece, (block + 1) * sub // piece):
                        copies[k].wait()
                for x in range(sub):
                    scratch[block % 2][x * stride:x * stride + y_local, :] = (
                        rows[block * sub + x].astype(f32)
                    )

            spread(0)
            for block in range(span * parts):
                if block + 1 < span * parts:
                    spread(block + 1)
                low = block * sub
                sums = None
                for y_cell in range(0, y_local, CELLS):
                    cells = []
                    for y_at in range(y_cell, y_cell + CELLS):
                        cell = scratch[block % 2][pl.ds(y_at, sub, stride=stride), :].astype(bf16)
                        flat[low:low + sub, y_at * z_local:(y_at + 1) * z_local] = cell
                        cells.append(cell)
                    parted = jnp.dot(
                        jnp.concatenate(cells, axis=0), table_z, preferred_element_type=f32
                    )
                    for k in range(CELLS):
                        part = parted[k * sub:(k + 1) * sub] * omega_y[y_cell + k:y_cell + k + 1, :]
                        sums = part if sums is None else sums + part
                if joined:
                    outs[0][low:low + sub, :] = sums
                else:
                    start = block % parts * sub
                    outs[block // parts][start:start + sub, :] = sums

        if opening:
            seeds_copy = pltpu.make_async_copy(seeds_hbm, seeds_ref, sems.at[len(copies)])
            seeds_copy.start()

        @pl.when(me >= 0)
        def compute():
            if opening:
                seeds_copy.wait()
                make_tables()
            make_rows()

        for copy in copies[total // piece if opening else 0:]:
            copy.wait()

    count = 1 if joined else span
    shape = held((total if joined else chunk, RANK), f32)
    out_shape = [shape] * count + [held((total, y_local * z_local), bf16)]
    scratch_shapes = [pltpu.VMEM(((sub + 1) * stride, z_local), f32)] * 2
    operands = [pltpu.with_memory_space_constraint(field, pltpu.HBM)]
    if follow:
        out_shape.append(held((len(follow) * chunk, y_local, z_local), bf16))
    if opening:
        operands.append(pltpu.with_memory_space_constraint(seeds, pltpu.HBM))
        in_specs = [HBM_SPACE, HBM_SPACE]
        out_shape += [held((z_local, RANK), bf16), held((y_local, RANK), f32)]
        scratch_shapes.append(pltpu.VMEM((total, y_local, z_local), bf16))
        scratch_shapes.append(pltpu.SMEM(seeds.shape, i32))
    else:
        operands += carried
        in_specs = [HBM_SPACE] + [VMEM_SPACE] * 3
    copies = (len(follow) + (span if opening else 0)) * (chunk // piece)
    scratch_shapes.append(pltpu.SemaphoreType.DMA((copies + 1,)))
    result = call(
        kernel, out_shape, in_specs,
        flops=2 * total * y_local * z_local * RANK, moved=2 * total * y_local * z_local,
        scratch_shapes=scratch_shapes,
    )(*operands)
    coming = list(result[count + 1:count + 2]) if follow else []
    tables = list(result[-2:]) if opening else carried[1:]
    return result[:count], result[count], coming + tables


def split3(value):
    high = value.astype(bf16)
    rest = value - high.astype(f32)
    middle = rest.astype(bf16)
    return high, middle, (rest - middle.astype(f32)).astype(bf16)


PANEL = 32
PIVOTS = 16


def inverse_factor_kernel(gram, came, out, state):
    size = gram.shape[0]
    state[...] = gram[...] + came[...]
    lane = lax.broadcasted_iota(i32, (8, 128), 1)
    row = lax.broadcasted_iota(i32, (8, 128), 0)
    zero = jnp.where(lane < 0, 1.0, 0.0).astype(f32)
    groups = PANEL // 8

    def over_rows(value, i):
        return jnp.broadcast_to(value[i:i + 1], (8, 128))

    def over_lanes(value, i):
        return jnp.broadcast_to(value[:, i:i + 1], (8, 128))

    for low in range(0, size, PANEL):
        high = low + PANEL
        tile, offset = low // 128, low % 128
        rows = [
            [state[low + 8 * q:low + 8 * q + 8, 128 * k:128 * k + 128] for q in range(groups)]
            for k in range(2)
        ]
        rows.append(
            [jnp.where(lane == row + (offset + 8 * q), 1.0, 0.0).astype(f32) for q in range(groups)]
        )
        done = [[None] * groups for _ in range(3)]
        scales = [jnp.zeros((8, 128), f32)] * groups
        ratios = [jnp.zeros((8, 128), f32)] * groups
        for base in range(0, PANEL, PIVOTS):
            column = [
                {q: over_lanes(rows[tile][q], offset + base + m) + zero for q in range(base // 8, groups)}
                for m in range(PIVOTS)
            ]
            for c in range(0, PIVOTS, 2):
                g, i = (base + c) // 8, c % 8
                d11, d12 = over_rows(column[c][g], i), over_rows(column[c + 1][g], i)
                d22 = over_rows(column[c + 1][g], i + 1)
                inverse = pl.reciprocal(d11 * d22 - d12 * d12)
                k11, k12, k22 = d22 * inverse, d12 * inverse, d11 * inverse
                ratio = d12 * pl.reciprocal(d11)
                root1, root2 = lax.rsqrt(d11), lax.rsqrt(d22 - ratio * d12)
                scales[g] = jnp.where(row == i, root1, jnp.where(row == i + 1, root2, scales[g]))
                ratios[g] = jnp.where(row == i + 1, ratio, ratios[g])
                left, right = dict(column[c]), dict(column[c + 1])
                left[g] = jnp.where(row > i + 1, left[g], 0.0)
                right[g] = jnp.where(row > i + 1, right[g], 0.0)
                start = g if i + 2 < 8 else g + 1
                for m in range(c + 2, PIVOTS):
                    a, b = over_rows(column[m][g], i), over_rows(column[m][g], i + 1)
                    first, second = k11 * a - k12 * b, k22 * b - k12 * a
                    for q in range(start, groups):
                        column[m][q] = column[m][q] - (left[q] * first + right[q] * second)
                for k in range(3):
                    a, b = over_rows(rows[k][g], i), over_rows(rows[k][g], i + 1)
                    first, second = k11 * a - k12 * b, k22 * b - k12 * a
                    for q in range(start, groups):
                        rows[k][q] = rows[k][q] - (left[q] * first + right[q] * second)
                if i == 6:
                    for k in range(3):
                        above = pltpu.roll(rows[k][g], 1, 0)
                        done[k][g] = (rows[k][g] - ratios[g] * above) * scales[g]
        factor = [jnp.concatenate(part, axis=0) for part in done]
        lanes = lax.broadcasted_iota(i32, (PANEL, 128), 1)
        inside = (lanes >= offset) & (lanes < offset + PANEL)
        mixed = list(factor[:2])
        mixed[tile] = jnp.where(inside, factor[2], factor[tile])
        for k in range(2):
            if k < tile:
                value = mixed[k]
            elif k == tile:
                value = jnp.where(lanes < offset + PANEL, mixed[k], 0.0)
            else:
                value = jnp.zeros((PANEL, 128), f32)
            out[low:high, 128 * k:128 * (k + 1)] = value
        if high < size:
            start = high // 128 * 128
            h, m, l = split3(jnp.concatenate(factor[:2], axis=1)[:, start:])
            eh, em, el = split3(jnp.concatenate(mixed, axis=1))
            left = jnp.concatenate([h, h, m, m, h, l], axis=0)
            right = jnp.concatenate([eh, em, eh, em, el, eh], axis=0)
            update = lax.dot_general(
                left, right, (((0,), (0,)), ((), ())), preferred_element_type=f32
            )
            columns = lax.broadcasted_iota(i32, (size - high, size), 1)
            rest = jnp.where((columns >= low) & (columns < high), 0.0, state[high:, :])
            state[high:, :] = rest - update[high - start:, :]


def inverse_factor(gram, came):
    return call(
        inverse_factor_kernel, held(gram.shape, f32), [VMEM_SPACE] * 2,
        flops=3 * gram.shape[0] ** 3, moved=8 * gram.shape[0] ** 2,
        scratch_shapes=[pltpu.VMEM(gram.shape, f32)],
    )(gram, came)


def merge(kept, came):
    chunk = kept[0].shape[0]

    def kernel(*refs):
        came_ref = refs[len(kept)]
        for k in range(len(kept)):
            refs[len(kept) + 1 + k][...] = refs[k][...] + came_ref[k * chunk:(k + 1) * chunk, :]

    return call(
        kernel, [held(kept[0].shape, f32)] * len(kept), [VMEM_SPACE] * (len(kept) + 1),
        flops=came.size, moved=12 * came.size,
    )(*kept, came)


def total_of(parts):
    def kernel(*refs):
        sums = refs[0][...]
        for ref in refs[1:-1]:
            sums = sums + ref[...]
        refs[-1][...] = sums

    return call(
        kernel, held(parts[0].shape, f32), [VMEM_SPACE] * len(parts),
        flops=parts[0].size * len(parts), moved=4 * parts[0].size * len(parts),
    )(*parts)


def gram_of(chunks):
    chunk = chunks[0].shape[0]
    total = len(chunks) * chunk

    def kernel(*refs):
        rows_refs, (out, terms) = refs[:-2], refs[-2:]
        for k, ref in enumerate(rows_refs):
            for j, term in enumerate(split3(ref[...])):
                terms[k * chunk:(k + 1) * chunk, j * RANK:(j + 1) * RANK] = term
        over_rows = (((0,), (0,)), ((), ()))
        first = lax.dot_general(
            terms[:, :RANK], terms[...], over_rows, preferred_element_type=f32
        )
        middle = terms[:, RANK:2 * RANK]
        second = lax.dot_general(middle, middle, over_rows, preferred_element_type=f32)
        mixed = first[:, RANK:2 * RANK] + first[:, 2 * RANK:]
        out[...] = first[:, :RANK] + (second + (mixed + mixed.T))

    return call(
        kernel, held((RANK, RANK), f32), [VMEM_SPACE] * len(chunks),
        flops=8 * total * RANK ** 2, moved=4 * total * RANK,
        scratch_shapes=[pltpu.VMEM((total, 3 * RANK), bf16)],
    )(*chunks)


def split2(value):
    high = value.astype(bf16)
    return high, (value - high.astype(f32)).astype(bf16)


def solve_rows(chunks, inverse, sizes, places):
    outer, inner, chunk = sizes
    total = len(chunks) * chunk
    half = RANK // 2

    def kernel(inverse_ref, *refs):
        rows_refs, (basis, turned, rounded) = refs[:-3], refs[-3:]
        me = lax.axis_index("yz")
        o, y = me // inner, me % inner
        high, low = split2(inverse_ref[...])
        right = jnp.concatenate([high, high, low], axis=1)
        for k in range(outer * inner):
            d, flip = k // inner, k % inner
            high, low = split2(rows_refs[k][...])
            left = jnp.concatenate([high, low, high], axis=1)
            value = lax.dot_general(left, right, (((1,), (1,)), ((), ())), preferred_element_type=f32)
            chosen = lax.rem(o + outer - d, outer) * inner + (inner - 1 - y if flip else y)
            basis[pl.ds(pl.multiple_of(chosen * chunk, chunk), chunk), :] = value
            rounded[places[k] * chunk:(places[k] + 1) * chunk, :] = value
        step = 128
        for start in range(0, total, step):
            block = rounded[start:start + step, :].T.astype(bf16)
            first = lax.axis_index("gx") == 0
            turned[:half, start:start + step] = jnp.where(first, block[half:], block[:half])
            turned[half:, start:start + step] = jnp.where(first, block[:half], block[half:])

    return call(
        kernel, [held((total, RANK), f32), held((RANK, total), bf16)],
        [VMEM_SPACE] * (1 + len(chunks)),
        flops=6 * total * RANK ** 2, moved=8 * total * RANK,
        scratch_shapes=[pltpu.VMEM((total, RANK), f32)],
    )(inverse, *chunks)


WIDTH = 256


def product(turned, flats, low, high, basis, first, stored):
    half = RANK // 2
    share = basis.shape[0] // PIECES

    def kernel(turned_ref, *refs):
        refs = list(refs)
        flat_refs = [refs.pop(0) for _ in flats]
        basis_ref = refs.pop(0)
        other, own, out, sem = refs[-4:]
        copy = pltpu.make_async_copy(
            basis_ref.at[pl.ds(first, share)], out.at[pl.ds(first, share)], sem
        )
        copy.start()

        @pl.when(lax.axis_index("yz") >= 0)
        def compute():
            for start in range(low, high, WIDTH):
                cells = jnp.concatenate([flat[:, start:start + WIDTH] for flat in flat_refs], axis=0)
                sums = jnp.dot(turned_ref[...], cells, preferred_element_type=f32)
                other[:, start - low:start - low + WIDTH] = sums[:half]
                own[:, start - low:start - low + WIDTH] = sums[half:]

        copy.wait()

    shape = (half, high - low)
    depth = turned.shape[1]
    operands = [turned, *flats, basis]
    in_specs = [VMEM_SPACE] * len(operands)
    more = {}
    if stored is not None:
        more["input_output_aliases"] = {len(operands): 2}
        operands.append(stored)
        in_specs.append(ANY_SPACE)
    return call(
        kernel,
        [held(shape, f32), held(shape, f32), pltpu.HBM(basis.shape, f32)], in_specs,
        flops=2 * RANK * depth * (high - low), moved=2 * depth * (high - low),
        out_specs=[VMEM_SPACE, VMEM_SPACE, HBM_SPACE],
        scratch_shapes=[pltpu.SemaphoreType.DMA], **more,
    )(*operands)


def finish(own, came, first, y_local, z_local, stored):
    half, columns = own.shape
    cells = columns // z_local
    stride = cells + 1

    def kernel(own_ref, came_ref, *refs):
        out, spread, rounded, sem = refs[-4:]
        for k in range(cells):
            at = k * z_local
            spread[pl.ds(k, half, stride=stride), :] = (
                own_ref[:, at:at + z_local] + came_ref[:, at:at + z_local]
            )
        for r in range(half):
            rounded[r] = spread[r * stride:r * stride + cells, :].astype(bf16)
        copy = pltpu.make_async_copy(rounded, out.at[:, pl.ds(first, cells)], sem)
        copy.start()
        copy.wait()

    operands, in_specs, more = [own, came], [VMEM_SPACE] * 2, {}
    if stored is not None:
        more["input_output_aliases"] = {2: 0}
        operands.append(stored)
        in_specs.append(ANY_SPACE)
    return call(
        kernel, pltpu.HBM((half, y_local, z_local), bf16), in_specs,
        out_specs=HBM_SPACE, moved=10 * own.size,
        scratch_shapes=[
            pltpu.VMEM(((half + 1) * stride, z_local), f32), pltpu.VMEM((half, cells, z_local), bf16),
            pltpu.SemaphoreType.DMA,
        ],
        **more,
    )(*operands)


def local(field, sketch_seeds):
    x_local, y_local, z_local = field.shape
    count = lax.axis_size("yz")
    inner = 2 if count % 2 == 0 else 1
    outer = count // inner
    chunk = x_local // count

    def neighbour(value):
        return lax.ppermute(value, "yz", [(i, i ^ 1) for i in range(count)])

    def shift(value, d):
        pairs = [(i, (i // inner + d) % outer * inner + i % inner) for i in range(count)]
        return lax.ppermute(value, "yz", pairs)

    def other_core(value):
        return lax.ppermute(value, "gx", [(0, 1), (1, 0)])

    sizes = (outer, inner, chunk)
    order = sorted(range(1, outer), key=lambda d: -min(d, outer - d)) + [0]
    groups = [group for group in (order[:1], order[1:-1], order[-1:] if outer > 1 else []) if group]
    turns = turns_of(len(groups), inner)
    pairs = [[(d, flip) for d in groups[k]] for k, flip in turns]
    wanted = [pair for some in pairs for pair in some]
    flats, sends, parts, carried = [], {}, [], None
    for turn, (k, flip) in enumerate(turns):
        follow = pairs[turn + 1] if turn + 1 < len(turns) else []
        made, flat, carried = sketch_chunks(
            field, sketch_seeds, pairs[turn], follow, sizes, flip == 1, carried
        )
        flats.append(flat)
        if flip:
            sends[k] = neighbour(made[0])
            continue
        kept = merge(made, sends[k]) if inner == 2 else made
        for j, d in enumerate(groups[k]):
            parts.append(shift(kept[j], d) if d else kept[j])
    own = total_of(parts)
    chunks = [None] * count
    near = [0] + sorted(range(1, outer), key=lambda d: min(d, outer - d))
    for d in near:
        came = shift(own, d) if d else own
        chunks[d * inner] = came
        if inner == 2:
            chunks[d * inner + 1] = neighbour(came)
    gram = gram_of(chunks)
    came = other_core(gram)
    inverse = inverse_factor(gram, came)
    places = [wanted.index(((outer - k // inner) % outer, k % inner)) for k in range(count)]
    basis, turned = solve_rows(chunks, inverse, sizes, places)
    columns = y_local * z_local
    stored, core, waiting = None, None, []
    for k in range(PIECES):
        other, mine, stored = product(
            turned, flats, columns * k // PIECES, columns * (k + 1) // PIECES,
            basis, x_local * k // PIECES, stored,
        )
        came = other_core(other)
        waiting.append((mine, came))
    for k, (mine, came) in enumerate(waiting):
        core = finish(mine, came, y_local * k // PIECES, y_local, z_local, core)
    return (stored, core)


PIECES = 4


def turns_of(groups, inner):
    if inner == 1:
        return [(k, 0) for k in range(groups)]
    if groups < 3:
        return [(k, 1) for k in range(groups)] + [(k, 0) for k in range(groups)]
    return [(0, 1), (1, 1), (0, 0), (2, 1), (1, 0), (2, 0)]


def solution(mesh):
    in_specs = (P(("grp", "gx"), "yz", None), P("grp"))
    out_specs = (P(("grp", "gx"), None), P(("grp", "gx"), "yz", None))

    return jax.shard_map(local, mesh=mesh, in_specs=in_specs, out_specs=out_specs, check_vma=False)
```

```python
import jax
import jax.numpy as jnp
from jax import lax
from jax.experimental import pallas as pl
from jax.experimental.pallas import tpu as pltpu
from jax.sharding import PartitionSpec as P

RANK = 256
prime = 32749
f32, bf16, i32 = jnp.float32, jnp.bfloat16, jnp.int32


def remainder(value):
    quotient = (value.astype(f32) * (1.0 / prime)).astype(i32)
    rest = value - quotient * prime
    rest = jnp.where(rest < 0, rest + prime, rest)
    return jnp.where(rest >= prime, rest - prime, rest)


def omega_table(a, b, c, start, count):
    place = start + 1 + lax.broadcasted_iota(i32, (count, 1), 0)
    column = 1 + lax.broadcasted_iota(i32, (1, RANK), 1)
    first = remainder(a * place)
    second = remainder(b * column + c)
    square = remainder(place * place)
    third = remainder(c * column)
    mixed = remainder(remainder(first * second) + remainder(square * third))
    return mixed.astype(f32) * (2.0 / prime) - 1.0


LIMIT = 14 << 20
VMEM_SPACE = pl.BlockSpec(memory_space=pltpu.VMEM)
ANY_SPACE = pl.BlockSpec(memory_space=pl.ANY)
HBM_SPACE = pl.BlockSpec(memory_space=pltpu.HBM)
SUB = 64


def held(shape, dtype):
    return pltpu.VMEM(shape, dtype)


def call(kernel, out_shape, in_specs, flops=0, moved=0, **more):
    return pl.pallas_call(
        kernel,
        out_shape=out_shape,
        in_specs=in_specs,
        compiler_params=pltpu.CompilerParams(vmem_limit_bytes=LIMIT),
        cost_estimate=pl.CostEstimate(flops=flops, bytes_accessed=moved, transcendentals=0),
        **more,
    )


CELLS = 4


def sketch_chunks(field, seeds, wanted, follow, sizes, joined, carried=None):
    outer, inner, chunk = sizes
    _, y_local, z_local = field.shape
    sub = min(SUB, chunk)
    stride = y_local + 1
    parts = chunk // sub
    piece = min(32, sub)
    span = len(wanted)
    total = span * chunk
    opening = carried is None

    def kernel(*refs):
        refs = list(refs)
        field_ref, sems = refs.pop(0), refs.pop()
        if opening:
            seeds_hbm, seeds_ref, rows = refs.pop(0), refs.pop(), refs.pop()
        else:
            rows, omega_z, omega_y = refs.pop(0), refs.pop(0), refs.pop(0)
        outs = [refs.pop(0) for _ in range(1 if joined else span)]
        flat = refs.pop(0)
        later = refs.pop(0) if follow else None
        if opening:
            omega_z, omega_y = refs.pop(0), refs.pop(0)
        me = lax.axis_index("yz")
        o, y = me // inner, me % inner
        moves = [(pair, rows, k) for k, pair in enumerate(wanted) if opening]
        moves += [(pair, later, k) for k, pair in enumerate(follow)]
        copies = []
        for (d, flip), target, k in moves:
            chosen = lax.rem(o + d, outer) * inner + (inner - 1 - y if flip else y)
            for start in range(0, chunk, piece):
                copy = pltpu.make_async_copy(
                    field_ref.at[pl.ds(chosen * chunk + start, piece)],
                    target.at[pl.ds(k * chunk + start, piece)],
                    sems.at[len(copies)],
                )
                copy.start()
                copies.append(copy)

        def make_tables():
            omega_z[...] = omega_table(
                seeds_ref[3], seeds_ref[4], seeds_ref[5], 0, z_local
            ).astype(bf16)
            omega_y[...] = omega_table(
                seeds_ref[0], seeds_ref[1], seeds_ref[2], me * y_local, y_local
            )

        def make_rows():
            scratch = refs
            table_z = omega_z[...]

            def spread(block):
                if opening:
                    for k in range(block * sub // piece, (block + 1) * sub // piece):
                        copies[k].wait()
                for x in range(sub):
                    scratch[block % 2][x * stride:x * stride + y_local, :] = (
                        rows[block * sub + x].astype(f32)
                    )

            spread(0)
            for block in range(span * parts):
                if block + 1 < span * parts:
                    spread(block + 1)
                low = block * sub
                sums = None
                for y_cell in range(0, y_local, CELLS):
                    cells = []
                    for y_at in range(y_cell, y_cell + CELLS):
                        cell = scratch[block % 2][pl.ds(y_at, sub, stride=stride), :].astype(bf16)
                        flat[low:low + sub, y_at * z_local:(y_at + 1) * z_local] = cell
                        cells.append(cell)
                    parted = jnp.dot(
                        jnp.concatenate(cells, axis=0), table_z, preferred_element_type=f32
                    )
                    for k in range(CELLS):
                        part = parted[k * sub:(k + 1) * sub] * omega_y[y_cell + k:y_cell + k + 1, :]
                        sums = part if sums is None else sums + part
                if joined:
                    outs[0][low:low + sub, :] = sums
                else:
                    start = block % parts * sub
                    outs[block // parts][start:start + sub, :] = sums

        if opening:
            seeds_copy = pltpu.make_async_copy(seeds_hbm, seeds_ref, sems.at[len(copies)])
            seeds_copy.start()

        @pl.when(me >= 0)
        def compute():
            if opening:
                seeds_copy.wait()
                make_tables()
            make_rows()

        for copy in copies[total // piece if opening else 0:]:
            copy.wait()

    count = 1 if joined else span
    shape = held((total if joined else chunk, RANK), f32)
    out_shape = [shape] * count + [held((total, y_local * z_local), bf16)]
    scratch_shapes = [pltpu.VMEM(((sub + 1) * stride, z_local), f32)] * 2
    operands = [pltpu.with_memory_space_constraint(field, pltpu.HBM)]
    if follow:
        out_shape.append(held((len(follow) * chunk, y_local, z_local), bf16))
    if opening:
        operands.append(pltpu.with_memory_space_constraint(seeds, pltpu.HBM))
        in_specs = [HBM_SPACE, HBM_SPACE]
        out_shape += [held((z_local, RANK), bf16), held((y_local, RANK), f32)]
        scratch_shapes.append(pltpu.VMEM((total, y_local, z_local), bf16))
        scratch_shapes.append(pltpu.SMEM(seeds.shape, i32))
    else:
        operands += carried
        in_specs = [HBM_SPACE] + [VMEM_SPACE] * 3
    copies = (len(follow) + (span if opening else 0)) * (chunk // piece)
    scratch_shapes.append(pltpu.SemaphoreType.DMA((copies + 1,)))
    result = call(
        kernel, out_shape, in_specs,
        flops=2 * total * y_local * z_local * RANK, moved=2 * total * y_local * z_local,
        scratch_shapes=scratch_shapes,
    )(*operands)
    coming = list(result[count + 1:count + 2]) if follow else []
    tables = list(result[-2:]) if opening else carried[1:]
    return result[:count], result[count], coming + tables


def split3(value):
    high = value.astype(bf16)
    rest = value - high.astype(f32)
    middle = rest.astype(bf16)
    return high, middle, (rest - middle.astype(f32)).astype(bf16)


PANEL = 32
PIVOTS = 16


def inverse_factor_kernel(gram, came, out, state):
    size = gram.shape[0]
    state[...] = gram[...] + came[...]
    lane = lax.broadcasted_iota(i32, (8, 128), 1)
    row = lax.broadcasted_iota(i32, (8, 128), 0)
    zero = jnp.where(lane < 0, 1.0, 0.0).astype(f32)
    groups = PANEL // 8

    def over_rows(value, i):
        return jnp.broadcast_to(value[i:i + 1], (8, 128))

    def over_lanes(value, i):
        return jnp.broadcast_to(value[:, i:i + 1], (8, 128))

    for low in range(0, size, PANEL):
        high = low + PANEL
        tile, offset = low // 128, low % 128
        rows = [
            [state[low + 8 * q:low + 8 * q + 8, 128 * k:128 * k + 128] for q in range(groups)]
            for k in range(2)
        ]
        rows.append(
            [jnp.where(lane == row + (offset + 8 * q), 1.0, 0.0).astype(f32) for q in range(groups)]
        )
        done = [[None] * groups for _ in range(3)]
        scales = [jnp.zeros((8, 128), f32)] * groups
        ratios = [jnp.zeros((8, 128), f32)] * groups
        for base in range(0, PANEL, PIVOTS):
            column = [
                {q: over_lanes(rows[tile][q], offset + base + m) + zero for q in range(base // 8, groups)}
                for m in range(PIVOTS)
            ]
            for c in range(0, PIVOTS, 2):
                g, i = (base + c) // 8, c % 8
                d11, d12 = over_rows(column[c][g], i), over_rows(column[c + 1][g], i)
                d22 = over_rows(column[c + 1][g], i + 1)
                inverse = pl.reciprocal(d11 * d22 - d12 * d12)
                k11, k12, k22 = d22 * inverse, d12 * inverse, d11 * inverse
                ratio = d12 * pl.reciprocal(d11)
                root1, root2 = lax.rsqrt(d11), lax.rsqrt(d22 - ratio * d12)
                scales[g] = jnp.where(row == i, root1, jnp.where(row == i + 1, root2, scales[g]))
                ratios[g] = jnp.where(row == i + 1, ratio, ratios[g])
                left, right = dict(column[c]), dict(column[c + 1])
                left[g] = jnp.where(row > i + 1, left[g], 0.0)
                right[g] = jnp.where(row > i + 1, right[g], 0.0)
                start = g if i + 2 < 8 else g + 1
                for m in range(c + 2, PIVOTS):
                    a, b = over_rows(column[m][g], i), over_rows(column[m][g], i + 1)
                    first, second = k11 * a - k12 * b, k22 * b - k12 * a
                    for q in range(start, groups):
                        column[m][q] = column[m][q] - (left[q] * first + right[q] * second)
                for k in range(3):
                    a, b = over_rows(rows[k][g], i), over_rows(rows[k][g], i + 1)
                    first, second = k11 * a - k12 * b, k22 * b - k12 * a
                    for q in range(start, groups):
                        rows[k][q] = rows[k][q] - (left[q] * first + right[q] * second)
                if i == 6:
                    for k in range(3):
                        above = pltpu.roll(rows[k][g], 1, 0)
                        done[k][g] = (rows[k][g] - ratios[g] * above) * scales[g]
        factor = [jnp.concatenate(part, axis=0) for part in done]
        lanes = lax.broadcasted_iota(i32, (PANEL, 128), 1)
        inside = (lanes >= offset) & (lanes < offset + PANEL)
        mixed = list(factor[:2])
        mixed[tile] = jnp.where(inside, factor[2], factor[tile])
        for k in range(2):
            if k < tile:
                value = mixed[k]
            elif k == tile:
                value = jnp.where(lanes < offset + PANEL, mixed[k], 0.0)
            else:
                value = jnp.zeros((PANEL, 128), f32)
            out[low:high, 128 * k:128 * (k + 1)] = value
        if high < size:
            start = high // 128 * 128
            h, m, l = split3(jnp.concatenate(factor[:2], axis=1)[:, start:])
            eh, em, el = split3(jnp.concatenate(mixed, axis=1))
            left = jnp.concatenate([h, h, m, m, h, l], axis=0)
            right = jnp.concatenate([eh, em, eh, em, el, eh], axis=0)
            update = lax.dot_general(
                left, right, (((0,), (0,)), ((), ())), preferred_element_type=f32
            )
            columns = lax.broadcasted_iota(i32, (size - high, size), 1)
            rest = jnp.where((columns >= low) & (columns < high), 0.0, state[high:, :])
            state[high:, :] = rest - update[high - start:, :]


def inverse_factor(gram, came):
    return call(
        inverse_factor_kernel, held(gram.shape, f32), [VMEM_SPACE] * 2,
        flops=3 * gram.shape[0] ** 3, moved=8 * gram.shape[0] ** 2,
        scratch_shapes=[pltpu.VMEM(gram.shape, f32)],
    )(gram, came)


def merge(kept, came):
    chunk = kept[0].shape[0]

    def kernel(*refs):
        came_ref = refs[len(kept)]
        for k in range(len(kept)):
            refs[len(kept) + 1 + k][...] = refs[k][...] + came_ref[k * chunk:(k + 1) * chunk, :]

    return call(
        kernel, [held(kept[0].shape, f32)] * len(kept), [VMEM_SPACE] * (len(kept) + 1),
        flops=came.size, moved=12 * came.size,
    )(*kept, came)


def total_of(parts):
    def kernel(*refs):
        sums = refs[0][...]
        for ref in refs[1:-1]:
            sums = sums + ref[...]
        refs[-1][...] = sums

    return call(
        kernel, held(parts[0].shape, f32), [VMEM_SPACE] * len(parts),
        flops=parts[0].size * len(parts), moved=4 * parts[0].size * len(parts),
    )(*parts)


def gram_of(chunks, base=None):
    chunk = chunks[0].shape[0]
    total = len(chunks) * chunk

    def kernel(*refs):
        rows_refs, (out, terms) = refs[:len(chunks)], refs[-2:]
        for k, ref in enumerate(rows_refs):
            for j, term in enumerate(split3(ref[...])):
                terms[k * chunk:(k + 1) * chunk, j * RANK:(j + 1) * RANK] = term
        over_rows = (((0,), (0,)), ((), ()))
        first = lax.dot_general(
            terms[:, :RANK], terms[...], over_rows, preferred_element_type=f32
        )
        middle = terms[:, RANK:2 * RANK]
        second = lax.dot_general(middle, middle, over_rows, preferred_element_type=f32)
        mixed = first[:, RANK:2 * RANK] + first[:, 2 * RANK:]
        sums = first[:, :RANK] + (second + (mixed + mixed.T))
        out[...] = sums if base is None else refs[len(chunks)][...] + sums

    operands = list(chunks) + ([] if base is None else [base])
    return call(
        kernel, held((RANK, RANK), f32), [VMEM_SPACE] * len(operands),
        flops=8 * total * RANK ** 2, moved=4 * total * RANK,
        scratch_shapes=[pltpu.VMEM((total, 3 * RANK), bf16)],
    )(*operands)


def split2(value):
    high = value.astype(bf16)
    return high, (value - high.astype(f32)).astype(bf16)


def solve_rows(chunks, inverse, sizes, places):
    outer, inner, chunk = sizes
    total = len(chunks) * chunk
    half = RANK // 2

    def kernel(inverse_ref, *refs):
        rows_refs, (basis, turned, rounded) = refs[:-3], refs[-3:]
        me = lax.axis_index("yz")
        o, y = me // inner, me % inner
        high, low = split2(inverse_ref[...])
        right = jnp.concatenate([high, high, low], axis=1)
        for k in range(outer * inner):
            d, flip = k // inner, k % inner
            high, low = split2(rows_refs[k][...])
            left = jnp.concatenate([high, low, high], axis=1)
            value = lax.dot_general(left, right, (((1,), (1,)), ((), ())), preferred_element_type=f32)
            chosen = lax.rem(o + outer - d, outer) * inner + (inner - 1 - y if flip else y)
            basis[pl.ds(pl.multiple_of(chosen * chunk, chunk), chunk), :] = value
            rounded[places[k] * chunk:(places[k] + 1) * chunk, :] = value
        step = 128
        for start in range(0, total, step):
            block = rounded[start:start + step, :].T.astype(bf16)
            first = lax.axis_index("gx") == 0
            turned[:half, start:start + step] = jnp.where(first, block[half:], block[:half])
            turned[half:, start:start + step] = jnp.where(first, block[:half], block[half:])

    return call(
        kernel, [held((total, RANK), f32), held((RANK, total), bf16)],
        [VMEM_SPACE] * (1 + len(chunks)),
        flops=6 * total * RANK ** 2, moved=8 * total * RANK,
        scratch_shapes=[pltpu.VMEM((total, RANK), f32)],
    )(inverse, *chunks)


WIDTH = 256


def product(turned, flats, low, high, basis, first, stored):
    half = RANK // 2
    share = basis.shape[0] // PIECES

    def kernel(turned_ref, *refs):
        refs = list(refs)
        flat_refs = [refs.pop(0) for _ in flats]
        basis_ref = refs.pop(0)
        other, own, out, sem = refs[-4:]
        copy = pltpu.make_async_copy(
            basis_ref.at[pl.ds(first, share)], out.at[pl.ds(first, share)], sem
        )
        copy.start()

        @pl.when(lax.axis_index("yz") >= 0)
        def compute():
            for start in range(low, high, WIDTH):
                cells = jnp.concatenate([flat[:, start:start + WIDTH] for flat in flat_refs], axis=0)
                sums = jnp.dot(turned_ref[...], cells, preferred_element_type=f32)
                other[:, start - low:start - low + WIDTH] = sums[:half]
                own[:, start - low:start - low + WIDTH] = sums[half:]

        copy.wait()

    shape = (half, high - low)
    depth = turned.shape[1]
    operands = [turned, *flats, basis]
    in_specs = [VMEM_SPACE] * len(operands)
    more = {}
    if stored is not None:
        more["input_output_aliases"] = {len(operands): 2}
        operands.append(stored)
        in_specs.append(ANY_SPACE)
    return call(
        kernel,
        [held(shape, f32), held(shape, f32), pltpu.HBM(basis.shape, f32)], in_specs,
        flops=2 * RANK * depth * (high - low), moved=2 * depth * (high - low),
        out_specs=[VMEM_SPACE, VMEM_SPACE, HBM_SPACE],
        scratch_shapes=[pltpu.SemaphoreType.DMA], **more,
    )(*operands)


def finish(own, came, y_local, z_local):
    half = own[0].shape[0]
    pieces = len(own)
    cells = y_local // pieces
    stride = y_local + 1
    step = min(half, 32)

    def kernel(*refs):
        out, spread, rounded, sems = refs[-4:]
        copies = []
        for start in range(0, half, step):
            for y_cell in range(y_local):
                k, at = y_cell // cells, y_cell % cells * z_local
                spread[pl.ds(start * stride + y_cell, step, stride=stride), :] = (
                    refs[k][start:start + step, at:at + z_local]
                    + refs[pieces + k][start:start + step, at:at + z_local]
                )
            for r in range(start, start + step):
                rounded[r] = spread[r * stride:r * stride + y_local, :].astype(bf16)
            copy = pltpu.make_async_copy(
                rounded.at[pl.ds(start, step)], out.at[pl.ds(start, step)], sems.at[start // step]
            )
            copy.start()
            copies.append(copy)
        for copy in copies:
            copy.wait()

    return call(
        kernel, pltpu.HBM((half, y_local, z_local), bf16), [VMEM_SPACE] * (2 * pieces),
        out_specs=HBM_SPACE, moved=10 * half * y_local * z_local,
        scratch_shapes=[
            pltpu.VMEM(((half + 1) * stride, z_local), f32),
            pltpu.VMEM((half, y_local, z_local), bf16),
            pltpu.SemaphoreType.DMA((half // step,)),
        ],
    )(*own, *came)


def local(field, sketch_seeds):
    x_local, y_local, z_local = field.shape
    count = lax.axis_size("yz")
    inner = 2 if count % 2 == 0 else 1
    outer = count // inner
    chunk = x_local // count

    def neighbour(value):
        return lax.ppermute(value, "yz", [(i, i ^ 1) for i in range(count)])

    def shift(value, d):
        pairs = [(i, (i // inner + d) % outer * inner + i % inner) for i in range(count)]
        return lax.ppermute(value, "yz", pairs)

    def other_core(value):
        return lax.ppermute(value, "gx", [(0, 1), (1, 0)])

    sizes = (outer, inner, chunk)
    order = sorted(range(1, outer), key=lambda d: -min(d, outer - d)) + [0]
    groups = [group for group in (order[:1], order[1:-1], order[-1:] if outer > 1 else []) if group]
    turns = turns_of(len(groups), inner)
    pairs = [[(d, flip) for d in groups[k]] for k, flip in turns]
    wanted = [pair for some in pairs for pair in some]
    flats, sends, parts, carried = [], {}, [], None
    for turn, (k, flip) in enumerate(turns):
        follow = pairs[turn + 1] if turn + 1 < len(turns) else []
        made, flat, carried = sketch_chunks(
            field, sketch_seeds, pairs[turn], follow, sizes, flip == 1, carried
        )
        flats.append(flat)
        if flip:
            sends[k] = neighbour(made[0])
            continue
        kept = merge(made, sends[k]) if inner == 2 else made
        for j, d in enumerate(groups[k]):
            parts.append(shift(kept[j], d) if d else kept[j])
    own = total_of(parts)
    chunks = [None] * count
    near = [0] + sorted(range(1, outer), key=lambda d: min(d, outer - d))
    for d in near:
        came = shift(own, d) if d else own
        chunks[d * inner] = came
        if inner == 2:
            chunks[d * inner + 1] = neighbour(came)
    late = [d * inner + 1 for d in near[-2:]] if early_gram(inner, outer) else []
    gram = None
    if late:
        gram = gram_of([chunks[k] for k in range(count) if k not in late])
    gram = gram_of([chunks[k] for k in late or range(count)], gram)
    came = other_core(gram)
    inverse = inverse_factor(gram, came)
    places = [wanted.index(((outer - k // inner) % outer, k % inner)) for k in range(count)]
    basis, turned = solve_rows(chunks, inverse, sizes, places)
    columns = y_local * z_local
    stored, mine, came = None, [], []
    for k in range(PIECES):
        other, own_part, stored = product(
            turned, flats, columns * k // PIECES, columns * (k + 1) // PIECES,
            basis, x_local * k // PIECES, stored,
        )
        came.append(other_core(other))
        mine.append(own_part)
    return (stored, finish(mine, came, y_local, z_local))


PIECES = 4


def early_gram(inner, outer):
    return inner == 2 and outer > 2


def turns_of(groups, inner):
    if inner == 1:
        return [(k, 0) for k in range(groups)]
    if groups < 3:
        return [(k, 1) for k in range(groups)] + [(k, 0) for k in range(groups)]
    return [(0, 1), (1, 1), (0, 0), (2, 1), (1, 0), (2, 0)]


def solution(mesh):
    in_specs = (P(("grp", "gx"), "yz", None), P("grp"))
    out_specs = (P(("grp", "gx"), None), P(("grp", "gx"), "yz", None))

    return jax.shard_map(local, mesh=mesh, in_specs=in_specs, out_specs=out_specs, check_vma=False)
```

```python
import jax
import jax.numpy as jnp
from jax import lax
from jax.experimental import pallas as pl
from jax.experimental.pallas import tpu as pltpu
from jax.sharding import PartitionSpec as P

RANK = 256
prime = 32749
f32, bf16, i32 = jnp.float32, jnp.bfloat16, jnp.int32


def remainder(value):
    quotient = (value.astype(f32) * (1.0 / prime)).astype(i32)
    rest = value - quotient * prime
    rest = jnp.where(rest < 0, rest + prime, rest)
    return jnp.where(rest >= prime, rest - prime, rest)


def omega_table(a, b, c, start, count):
    place = start + 1 + lax.broadcasted_iota(i32, (count, 1), 0)
    column = 1 + lax.broadcasted_iota(i32, (1, RANK), 1)
    first = remainder(a * place)
    second = remainder(b * column + c)
    square = remainder(place * place)
    third = remainder(c * column)
    mixed = remainder(remainder(first * second) + remainder(square * third))
    return mixed.astype(f32) * (2.0 / prime) - 1.0


LIMIT = 14 << 20
VMEM_SPACE = pl.BlockSpec(memory_space=pltpu.VMEM)
ANY_SPACE = pl.BlockSpec(memory_space=pl.ANY)
HBM_SPACE = pl.BlockSpec(memory_space=pltpu.HBM)
SUB = 64


def held(shape, dtype):
    return pltpu.VMEM(shape, dtype)


def call(kernel, out_shape, in_specs, flops=0, moved=0, **more):
    return pl.pallas_call(
        kernel,
        out_shape=out_shape,
        in_specs=in_specs,
        compiler_params=pltpu.CompilerParams(vmem_limit_bytes=LIMIT),
        cost_estimate=pl.CostEstimate(flops=flops, bytes_accessed=moved, transcendentals=0),
        **more,
    )


CELLS = 4


def sketch_chunks(field, seeds, wanted, follow, sizes, joined, carried=None):
    outer, inner, chunk = sizes
    _, y_local, z_local = field.shape
    sub = min(SUB, chunk)
    stride = y_local + 1
    parts = chunk // sub
    piece = min(32, sub)
    span = len(wanted)
    total = span * chunk
    opening = carried is None

    def kernel(*refs):
        refs = list(refs)
        field_ref, sems = refs.pop(0), refs.pop()
        if opening:
            seeds_hbm, seeds_ref, rows = refs.pop(0), refs.pop(), refs.pop()
        else:
            rows, omega_z, omega_y = refs.pop(0), refs.pop(0), refs.pop(0)
        outs = [refs.pop(0) for _ in range(1 if joined else span)]
        flat = refs.pop(0)
        later = refs.pop(0) if follow else None
        if opening:
            omega_z, omega_y = refs.pop(0), refs.pop(0)
        me = lax.axis_index("yz")
        o, y = me // inner, me % inner
        moves = [(pair, rows, k) for k, pair in enumerate(wanted) if opening]
        moves += [(pair, later, k) for k, pair in enumerate(follow)]
        copies = []
        for (d, flip), target, k in moves:
            chosen = lax.rem(o + d, outer) * inner + (inner - 1 - y if flip else y)
            for start in range(0, chunk, piece):
                copy = pltpu.make_async_copy(
                    field_ref.at[pl.ds(chosen * chunk + start, piece)],
                    target.at[pl.ds(k * chunk + start, piece)],
                    sems.at[len(copies)],
                )
                copy.start()
                copies.append(copy)

        def make_tables():
            omega_z[...] = omega_table(
                seeds_ref[3], seeds_ref[4], seeds_ref[5], 0, z_local
            ).astype(bf16)
            omega_y[...] = omega_table(
                seeds_ref[0], seeds_ref[1], seeds_ref[2], me * y_local, y_local
            )

        def make_rows():
            scratch = refs
            table_z = omega_z[...]

            def spread(block):
                if opening:
                    for k in range(block * sub // piece, (block + 1) * sub // piece):
                        copies[k].wait()
                for x in range(sub):
                    scratch[block % 2][x * stride:x * stride + y_local, :] = (
                        rows[block * sub + x].astype(f32)
                    )

            spread(0)
            for block in range(span * parts):
                if block + 1 < span * parts:
                    spread(block + 1)
                low = block * sub
                sums = None
                for y_cell in range(0, y_local, CELLS):
                    cells = []
                    for y_at in range(y_cell, y_cell + CELLS):
                        cell = scratch[block % 2][pl.ds(y_at, sub, stride=stride), :].astype(bf16)
                        flat[low:low + sub, y_at * z_local:(y_at + 1) * z_local] = cell
                        cells.append(cell)
                    parted = jnp.dot(
                        jnp.concatenate(cells, axis=0), table_z, preferred_element_type=f32
                    )
                    for k in range(CELLS):
                        part = parted[k * sub:(k + 1) * sub] * omega_y[y_cell + k:y_cell + k + 1, :]
                        sums = part if sums is None else sums + part
                if joined:
                    outs[0][low:low + sub, :] = sums
                else:
                    start = block % parts * sub
                    outs[block // parts][start:start + sub, :] = sums

        if opening:
            seeds_copy = pltpu.make_async_copy(seeds_hbm, seeds_ref, sems.at[len(copies)])
            seeds_copy.start()

        @pl.when(me >= 0)
        def compute():
            if opening:
                seeds_copy.wait()
                make_tables()
            make_rows()

        for copy in copies[total // piece if opening else 0:]:
            copy.wait()

    count = 1 if joined else span
    shape = held((total if joined else chunk, RANK), f32)
    out_shape = [shape] * count + [held((total, y_local * z_local), bf16)]
    scratch_shapes = [pltpu.VMEM(((sub + 1) * stride, z_local), f32)] * 2
    operands = [pltpu.with_memory_space_constraint(field, pltpu.HBM)]
    if follow:
        out_shape.append(held((len(follow) * chunk, y_local, z_local), bf16))
    if opening:
        operands.append(pltpu.with_memory_space_constraint(seeds, pltpu.HBM))
        in_specs = [HBM_SPACE, HBM_SPACE]
        out_shape += [held((z_local, RANK), bf16), held((y_local, RANK), f32)]
        scratch_shapes.append(pltpu.VMEM((total, y_local, z_local), bf16))
        scratch_shapes.append(pltpu.SMEM(seeds.shape, i32))
    else:
        operands += carried
        in_specs = [HBM_SPACE] + [VMEM_SPACE] * 3
    copies = (len(follow) + (span if opening else 0)) * (chunk // piece)
    scratch_shapes.append(pltpu.SemaphoreType.DMA((copies + 1,)))
    result = call(
        kernel, out_shape, in_specs,
        flops=2 * total * y_local * z_local * RANK, moved=2 * total * y_local * z_local,
        scratch_shapes=scratch_shapes,
    )(*operands)
    coming = list(result[count + 1:count + 2]) if follow else []
    tables = list(result[-2:]) if opening else carried[1:]
    return result[:count], result[count], coming + tables


def split3(value):
    high = value.astype(bf16)
    rest = value - high.astype(f32)
    middle = rest.astype(bf16)
    return high, middle, (rest - middle.astype(f32)).astype(bf16)


PANEL = 32
PIVOTS = 16


def inverse_factor_kernel(gram, came, out, state):
    size = gram.shape[0]
    state[...] = gram[...] + came[...]
    lane = lax.broadcasted_iota(i32, (8, 128), 1)
    row = lax.broadcasted_iota(i32, (8, 128), 0)
    zero = jnp.where(lane < 0, 1.0, 0.0).astype(f32)
    groups = PANEL // 8

    def over_rows(value, i):
        return jnp.broadcast_to(value[i:i + 1], (8, 128))

    def over_lanes(value, i):
        return jnp.broadcast_to(value[:, i:i + 1], (8, 128))

    for low in range(0, size, PANEL):
        high = low + PANEL
        tile, offset = low // 128, low % 128
        rows = [
            [state[low + 8 * q:low + 8 * q + 8, 128 * k:128 * k + 128] for q in range(groups)]
            for k in range(2)
        ]
        rows.append(
            [jnp.where(lane == row + (offset + 8 * q), 1.0, 0.0).astype(f32) for q in range(groups)]
        )
        done = [[None] * groups for _ in range(3)]
        scales = [jnp.zeros((8, 128), f32)] * groups
        ratios = [jnp.zeros((8, 128), f32)] * groups
        for base in range(0, PANEL, PIVOTS):
            column = [
                {q: over_lanes(rows[tile][q], offset + base + m) + zero for q in range(base // 8, groups)}
                for m in range(PIVOTS)
            ]
            for c in range(0, PIVOTS, 2):
                g, i = (base + c) // 8, c % 8
                d11, d12 = over_rows(column[c][g], i), over_rows(column[c + 1][g], i)
                d22 = over_rows(column[c + 1][g], i + 1)
                inverse = pl.reciprocal(d11 * d22 - d12 * d12)
                k11, k12, k22 = d22 * inverse, d12 * inverse, d11 * inverse
                ratio = d12 * pl.reciprocal(d11)
                root1, root2 = lax.rsqrt(d11), lax.rsqrt(d22 - ratio * d12)
                scales[g] = jnp.where(row == i, root1, jnp.where(row == i + 1, root2, scales[g]))
                ratios[g] = jnp.where(row == i + 1, ratio, ratios[g])
                left, right = dict(column[c]), dict(column[c + 1])
                left[g] = jnp.where(row > i + 1, left[g], 0.0)
                right[g] = jnp.where(row > i + 1, right[g], 0.0)
                start = g if i + 2 < 8 else g + 1
                for m in range(c + 2, PIVOTS):
                    a, b = over_rows(column[m][g], i), over_rows(column[m][g], i + 1)
                    first, second = k11 * a - k12 * b, k22 * b - k12 * a
                    for q in range(start, groups):
                        column[m][q] = column[m][q] - (left[q] * first + right[q] * second)
                for k in range(3):
                    a, b = over_rows(rows[k][g], i), over_rows(rows[k][g], i + 1)
                    first, second = k11 * a - k12 * b, k22 * b - k12 * a
                    for q in range(start, groups):
                        rows[k][q] = rows[k][q] - (left[q] * first + right[q] * second)
                if i == 6:
                    for k in range(3):
                        above = pltpu.roll(rows[k][g], 1, 0)
                        done[k][g] = (rows[k][g] - ratios[g] * above) * scales[g]
        factor = [jnp.concatenate(part, axis=0) for part in done]
        lanes = lax.broadcasted_iota(i32, (PANEL, 128), 1)
        inside = (lanes >= offset) & (lanes < offset + PANEL)
        mixed = list(factor[:2])
        mixed[tile] = jnp.where(inside, factor[2], factor[tile])
        for k in range(2):
            if k < tile:
                value = mixed[k]
            elif k == tile:
                value = jnp.where(lanes < offset + PANEL, mixed[k], 0.0)
            else:
                value = jnp.zeros((PANEL, 128), f32)
            out[low:high, 128 * k:128 * (k + 1)] = value
        if high < size:
            start = high // 128 * 128
            h, m, l = split3(jnp.concatenate(factor[:2], axis=1)[:, start:])
            eh, em, el = split3(jnp.concatenate(mixed, axis=1))
            left = jnp.concatenate([h, h, m, m, h, l], axis=0)
            right = jnp.concatenate([eh, em, eh, em, el, eh], axis=0)
            update = lax.dot_general(
                left, right, (((0,), (0,)), ((), ())), preferred_element_type=f32
            )
            columns = lax.broadcasted_iota(i32, (size - high, size), 1)
            rest = jnp.where((columns >= low) & (columns < high), 0.0, state[high:, :])
            state[high:, :] = rest - update[high - start:, :]


def inverse_factor(gram, came):
    return call(
        inverse_factor_kernel, held(gram.shape, f32), [VMEM_SPACE] * 2,
        flops=3 * gram.shape[0] ** 3, moved=8 * gram.shape[0] ** 2,
        scratch_shapes=[pltpu.VMEM(gram.shape, f32)],
    )(gram, came)


def merge(kept, came):
    chunk = kept[0].shape[0]

    def kernel(*refs):
        came_ref = refs[len(kept)]
        for k in range(len(kept)):
            refs[len(kept) + 1 + k][...] = refs[k][...] + came_ref[k * chunk:(k + 1) * chunk, :]

    return call(
        kernel, [held(kept[0].shape, f32)] * len(kept), [VMEM_SPACE] * (len(kept) + 1),
        flops=came.size, moved=12 * came.size,
    )(*kept, came)


def total_of(parts, cut):
    chunk = parts[0].shape[0]
    half = chunk // 2

    def kernel(*refs):
        sums = refs[0][...]
        for ref in refs[1:len(parts)]:
            sums = sums + ref[...]
        outs = refs[len(parts):]
        outs[0][...] = sums
        if cut:
            outs[1][...] = sums[:half]
            outs[2][...] = sums[half:]

    shapes = [(chunk, RANK)] + ([(half, RANK)] * 2 if cut else [])
    return call(
        kernel, [held(shape, f32) for shape in shapes], [VMEM_SPACE] * len(parts),
        flops=parts[0].size * len(parts), moved=4 * parts[0].size * len(parts),
    )(*parts)


def gram_of(chunks, base=None):
    total = sum(rows.shape[0] for rows in chunks)

    def kernel(*refs):
        rows_refs, (out, terms) = refs[:len(chunks)], refs[-2:]
        at = 0
        for ref in rows_refs:
            for j, term in enumerate(split3(ref[...])):
                terms[at:at + ref.shape[0], j * RANK:(j + 1) * RANK] = term
            at += ref.shape[0]
        over_rows = (((0,), (0,)), ((), ()))
        first = lax.dot_general(
            terms[:, :RANK], terms[...], over_rows, preferred_element_type=f32
        )
        middle = terms[:, RANK:2 * RANK]
        second = lax.dot_general(middle, middle, over_rows, preferred_element_type=f32)
        mixed = first[:, RANK:2 * RANK] + first[:, 2 * RANK:]
        sums = first[:, :RANK] + (second + (mixed + mixed.T))
        out[...] = sums if base is None else refs[len(chunks)][...] + sums

    operands = list(chunks) + ([] if base is None else [base])
    return call(
        kernel, held((RANK, RANK), f32), [VMEM_SPACE] * len(operands),
        flops=8 * total * RANK ** 2, moved=4 * total * RANK,
        scratch_shapes=[pltpu.VMEM((total, 3 * RANK), bf16)],
    )(*operands)


def split2(value):
    high = value.astype(bf16)
    return high, (value - high.astype(f32)).astype(bf16)


def solve_rows(pieces, inverse, sizes, places):
    outer, inner, chunk = sizes
    total = outer * inner * chunk
    half = RANK // 2

    def kernel(inverse_ref, *refs):
        rows_refs, (basis, turned, rounded) = refs[:-3], refs[-3:]
        me = lax.axis_index("yz")
        o, y = me // inner, me % inner
        high, low = split2(inverse_ref[...])
        right = jnp.concatenate([high, high, low], axis=1)
        for (k, begin, _), ref in zip(pieces, rows_refs):
            d, flip, size = k // inner, k % inner, ref.shape[0]
            high, low = split2(ref[...])
            left = jnp.concatenate([high, low, high], axis=1)
            value = lax.dot_general(left, right, (((1,), (1,)), ((), ())), preferred_element_type=f32)
            chosen = lax.rem(o + outer - d, outer) * inner + (inner - 1 - y if flip else y)
            basis[pl.ds(pl.multiple_of(chosen * chunk + begin, size), size), :] = value
            spot = places[k] * chunk + begin
            rounded[spot:spot + size, :] = value
        step = 128
        for start in range(0, total, step):
            block = rounded[start:start + step, :].T.astype(bf16)
            first = lax.axis_index("gx") == 0
            turned[:half, start:start + step] = jnp.where(first, block[half:], block[:half])
            turned[half:, start:start + step] = jnp.where(first, block[:half], block[half:])

    return call(
        kernel, [held((total, RANK), f32), held((RANK, total), bf16)],
        [VMEM_SPACE] * (1 + len(pieces)),
        flops=6 * total * RANK ** 2, moved=8 * total * RANK,
        scratch_shapes=[pltpu.VMEM((total, RANK), f32)],
    )(inverse, *[rows for _, _, rows in pieces])


WIDTH = 256


def product(turned, flats, low, high, basis, first, stored):
    half = RANK // 2
    share = basis.shape[0] // PIECES

    def kernel(turned_ref, *refs):
        refs = list(refs)
        flat_refs = [refs.pop(0) for _ in flats]
        basis_ref = refs.pop(0)
        other, own, out, sem = refs[-4:]
        copy = pltpu.make_async_copy(
            basis_ref.at[pl.ds(first, share)], out.at[pl.ds(first, share)], sem
        )
        copy.start()

        @pl.when(lax.axis_index("yz") >= 0)
        def compute():
            for start in range(low, high, WIDTH):
                cells = jnp.concatenate([flat[:, start:start + WIDTH] for flat in flat_refs], axis=0)
                sums = jnp.dot(turned_ref[...], cells, preferred_element_type=f32)
                other[:, start - low:start - low + WIDTH] = sums[:half]
                own[:, start - low:start - low + WIDTH] = sums[half:]

        copy.wait()

    shape = (half, high - low)
    depth = turned.shape[1]
    operands = [turned, *flats, basis]
    in_specs = [VMEM_SPACE] * len(operands)
    more = {}
    if stored is not None:
        more["input_output_aliases"] = {len(operands): 2}
        operands.append(stored)
        in_specs.append(ANY_SPACE)
    return call(
        kernel,
        [held(shape, f32), held(shape, f32), pltpu.HBM(basis.shape, f32)], in_specs,
        flops=2 * RANK * depth * (high - low), moved=2 * depth * (high - low),
        out_specs=[VMEM_SPACE, VMEM_SPACE, HBM_SPACE],
        scratch_shapes=[pltpu.SemaphoreType.DMA], **more,
    )(*operands)


def finish(own, came, y_local, z_local):
    half = own[0].shape[0]
    pieces = len(own)
    cells = y_local // pieces
    stride = y_local + 1
    step = min(half, 32)

    def kernel(*refs):
        out, spread, rounded, sems = refs[-4:]
        copies = []
        for start in range(0, half, step):
            for y_cell in range(y_local):
                k, at = y_cell // cells, y_cell % cells * z_local
                spread[pl.ds(start * stride + y_cell, step, stride=stride), :] = (
                    refs[k][start:start + step, at:at + z_local]
                    + refs[pieces + k][start:start + step, at:at + z_local]
                )
            for r in range(start, start + step):
                rounded[r] = spread[r * stride:r * stride + y_local, :].astype(bf16)
            copy = pltpu.make_async_copy(
                rounded.at[pl.ds(start, step)], out.at[pl.ds(start, step)], sems.at[start // step]
            )
            copy.start()
            copies.append(copy)
        for copy in copies:
            copy.wait()

    return call(
        kernel, pltpu.HBM((half, y_local, z_local), bf16), [VMEM_SPACE] * (2 * pieces),
        out_specs=HBM_SPACE, moved=10 * half * y_local * z_local,
        scratch_shapes=[
            pltpu.VMEM(((half + 1) * stride, z_local), f32),
            pltpu.VMEM((half, y_local, z_local), bf16),
            pltpu.SemaphoreType.DMA((half // step,)),
        ],
    )(*own, *came)


def local(field, sketch_seeds):
    x_local, y_local, z_local = field.shape
    count = lax.axis_size("yz")
    inner = 2 if count % 2 == 0 else 1
    outer = count // inner
    chunk = x_local // count

    def neighbour(value):
        return lax.ppermute(value, "yz", [(i, i ^ 1) for i in range(count)])

    def shift(value, d):
        pairs = [(i, (i // inner + d) % outer * inner + i % inner) for i in range(count)]
        return lax.ppermute(value, "yz", pairs)

    def other_core(value):
        return lax.ppermute(value, "gx", [(0, 1), (1, 0)])

    sizes = (outer, inner, chunk)
    order = sorted(range(1, outer), key=lambda d: -min(d, outer - d)) + [0]
    groups = [group for group in (order[:1], order[1:-1], order[-1:] if outer > 1 else []) if group]
    turns = turns_of(len(groups), inner)
    pairs = [[(d, flip) for d in groups[k]] for k, flip in turns]
    wanted = [pair for some in pairs for pair in some]
    flats, sends, parts, carried = [], {}, [], None
    for turn, (k, flip) in enumerate(turns):
        follow = pairs[turn + 1] if turn + 1 < len(turns) else []
        made, flat, carried = sketch_chunks(
            field, sketch_seeds, pairs[turn], follow, sizes, flip == 1, carried
        )
        flats.append(flat)
        if flip:
            sends[k] = neighbour(made[0])
            continue
        kept = merge(made, sends[k]) if inner == 2 else made
        for j, d in enumerate(groups[k]):
            parts.append(shift(kept[j], d) if d else kept[j])
    cut = early_gram(inner, outer)
    own, *halves = total_of(parts, cut)
    near = [0] + sorted(range(1, outer), key=lambda d: min(d, outer - d))
    sent = [(d, 0, own) for d in near[:-1 if cut else None]]
    sent += [(near[-1], k * chunk // 2, half) for k, half in enumerate(halves)]
    gathered, early = [], []
    for k, (d, begin, rows) in enumerate(sent):
        came = shift(rows, d) if d else rows
        gathered.append((d * inner, begin, came))
        early.append(True)
        if inner == 2:
            gathered.append((d * inner + 1, begin, neighbour(came)))
            early.append(k < outer - 2)
    gram = None
    if early_gram(inner, outer):
        gram = gram_of([rows for (_, _, rows), now in zip(gathered, early) if now])
        gram = gram_of([rows for (_, _, rows), now in zip(gathered, early) if not now], gram)
    else:
        gram = gram_of([rows for _, _, rows in gathered])
    came = other_core(gram)
    inverse = inverse_factor(gram, came)
    places = [wanted.index(((outer - k // inner) % outer, k % inner)) for k in range(count)]
    basis, turned = solve_rows(gathered, inverse, sizes, places)
    columns = y_local * z_local
    stored, mine, came = None, [], []
    for k in range(PIECES):
        other, own_part, stored = product(
            turned, flats, columns * k // PIECES, columns * (k + 1) // PIECES,
            basis, x_local * k // PIECES, stored,
        )
        came.append(other_core(other))
        mine.append(own_part)
    return (stored, finish(mine, came, y_local, z_local))


PIECES = 4


def early_gram(inner, outer):
    return inner == 2 and outer > 2


def turns_of(groups, inner):
    if inner == 1:
        return [(k, 0) for k in range(groups)]
    if groups < 3:
        return [(k, 1) for k in range(groups)] + [(k, 0) for k in range(groups)]
    return [(0, 1), (1, 1), (0, 0), (2, 1), (1, 0), (2, 0)]


def solution(mesh):
    in_specs = (P(("grp", "gx"), "yz", None), P("grp"))
    out_specs = (P(("grp", "gx"), None), P(("grp", "gx"), "yz", None))

    return jax.shard_map(local, mesh=mesh, in_specs=in_specs, out_specs=out_specs, check_vma=False)
```
